128 devices in a mesh: rows: 8 (over x_hi, z), cols: 16 (over x_lo, y, core).
Axes of the slice: x: 4 (x_hi: 2, x_lo: 2; x = x_hi * 2 + x_lo), y: 4, z: 4, core: 2. Of those that a mesh axis runs over, the one named last changes fastest.
Arguments:
- observed: float32 [426, 128, 2048], P(None, 'rows', 'cols'), may hold values from 0.05 to 3
- nonlin: float32 [128, 2048], P('rows', 'cols'), may hold values from -0.3 to 0.3
- abundance: float32 [64, 128, 2048], P(None, 'rows', 'cols'), may hold values from 0 to 2
- spectra: float32 [426, 64], replicated, may hold values from 0.1 to 1
- kernels: float32 [8, 9, 9], replicated, may hold values from 0.003 to 0.03
- tile_family: int32 [8, 16], P('rows', 'cols'), may hold values from 0 to 7
Outputs:
- abundance_out: float32 [64, 128, 2048], P(None, 'rows', 'cols')
- spectra_out: float32 [426, 64], replicated
The draws below stay inside these ranges and needn't reach their ends.
All inputs are finite; a program needn't handle non-finite values.
Results may differ from the reference program's by a relative error of at most 0.0003.
Values sent between devices are 32-bit elements; how exact they have to be, the bound alone decides.
A program may use at most 64 MiB of HBM per device.

```python
import math
import jax
import jax.numpy as jnp
from jax import lax

L = 426
P_SIZE = 64
KS = 9
FAMILIES = 8
ITERS = 3
CH = 16
CW = 128
NH = 128
NW = 2048
TILE_ROWS = 8
TILE_COLS = 16


def draw_observed(key, part):
    row_ramp = jnp.arange(NH, dtype=jnp.float32)[:, None] / NH
    col_ramp = jnp.arange(NW, dtype=jnp.float32)[None, :] / NW
    shading = 1.0 + row_ramp + col_ramp
    base = jnp.exp(jax.random.uniform(key, (L, NH, NW), jnp.float32, math.log(0.05), 0.0))
    return base * shading[None]


def plant(values, key, low, high):
    extent = values.shape
    spot = [jax.random.randint(jax.random.fold_in(key, axis), (), 0, extent[axis]) for axis in range(len(extent))]
    values = values.at[tuple(spot)].set(low)
    longest = extent.index(max(extent))
    spot[longest] = (spot[longest] + 1) % extent[longest]
    return values.at[tuple(spot)].set(high)


def block_levels(key, dims, split, smallest, largest):
    def one(position, shards_of):
        draws = jax.random.uniform(jax.random.fold_in(jax.random.fold_in(key, 6), position), (shards_of,), jnp.float32, smallest / len(split), largest / len(split))
        return jnp.repeat(jnp.exp(draws), dims[position] // shards_of).reshape((-1,) + (1,) * (len(dims) - position - 1))

    loudness = one(*split[0])
    for cut in split[1:]:
        loudness = loudness * one(*cut)
    return loudness


def setup_inputs(seed: int = 0) -> dict:
    key_list = jax.random.split(jax.random.key(seed), 7)
    return {
        "observed": draw_observed(jax.random.fold_in(key_list[6], 71), 0),
        "nonlin": jnp.clip(jax.random.uniform(key_list[1], (NH, NW), jnp.float32, -0.3, 0.3) * block_levels(key_list[1], (NH, NW), ((0, 8), (1, 16)), -0.4, 0.0), -0.3, 0.3),
        "abundance": jnp.clip(2.0 * jax.random.uniform(key_list[2], (P_SIZE, NH, NW), jnp.float32) ** block_levels(key_list[2], (P_SIZE, NH, NW), ((1, 8), (2, 16)), -0.2, 0.2), 0.0, 2.0),
        "spectra": jnp.clip(jax.random.uniform(key_list[3], (L, P_SIZE), jnp.float32, 0.1, 1.0), 0.1, 1.0),
        "kernels": jnp.clip(jnp.exp(jax.random.uniform(key_list[4], (FAMILIES, KS, KS), jnp.float32, math.log(0.003), math.log(0.03))), 0.003, 0.03),
        "tile_family": plant(jax.random.randint(key_list[5], (TILE_ROWS, TILE_COLS), 0, FAMILIES), jax.random.fold_in(key_list[5], 1), 0, FAMILIES - 1).astype(jnp.int32),
    }


def blur(abundance, tile_family, kernels):
    radius = KS // 2
    family_map = jnp.repeat(jnp.repeat(tile_family, CH, axis=0), CW, axis=1)
    table = kernels.reshape(kernels.shape[0], KS * KS)
    padded = jnp.pad(abundance, ((0, 0), (radius, radius), (radius, radius)))

    def add_tap(total, tap):
        row_shift = tap // KS
        col_shift = tap % KS
        column = lax.dynamic_slice_in_dim(table, tap, 1, 1)[:, 0]
        weight_map = jnp.take(column, family_map, axis=0)
        window = lax.dynamic_slice(padded, (jnp.int32(0), row_shift, col_shift), (P_SIZE, NH, NW))
        return (total + weight_map[None] * window, None)
    start = jnp.zeros((P_SIZE, NH, NW), jnp.float32)
    total, _ = lax.scan(add_tap, start, jnp.arange(KS * KS, dtype=jnp.int32))
    return total

def spectral(observed, nonlin, blurred, spectra):
    highest = lax.Precision.HIGHEST

    def strip(carry, index):
        start = index * CH
        pixels = lax.dynamic_slice_in_dim(observed, start, CH, 1).reshape(L, CH * NW)
        maps = lax.dynamic_slice_in_dim(blurred, start, CH, 1).reshape(P_SIZE, CH * NW)
        bend = lax.dynamic_slice_in_dim(nonlin, start, CH, 0).reshape(CH * NW)
        linear = jnp.dot(spectra, maps, precision=highest, preferred_element_type=jnp.float32) / P_SIZE
        resid = linear + bend[None] * linear * linear - pixels
        weighted = resid * (1.0 + 2.0 * bend[None] * linear)
        grad_flat = jnp.dot(spectra.T, weighted, precision=highest, preferred_element_type=jnp.float32) / P_SIZE
        part = jnp.dot(weighted, maps.T, precision=highest, preferred_element_type=jnp.float32) / P_SIZE
        return (carry + part, grad_flat.reshape(P_SIZE, CH, NW))
    start = jnp.zeros((L, P_SIZE), jnp.float32)
    total, strips = lax.scan(strip, start, jnp.arange(NH // CH, dtype=jnp.int32))
    grad_blur = jnp.transpose(strips, (1, 0, 2, 3)).reshape(P_SIZE, NH, NW)
    return (grad_blur, total)

def reference(observed, nonlin, abundance, spectra, kernels, tile_family):
    current = abundance
    endmembers = spectra
    pixel_count = NH * NW
    for step in range(ITERS):
        blurred, adjoint_fn = jax.vjp(lambda maps: blur(maps, tile_family, kernels), current)
        grad_blur, grad_spectra = spectral(observed, nonlin, blurred, endmembers)
        grad_abund = adjoint_fn(grad_blur)[0]
        current = jnp.maximum(current - 0.5 * grad_abund, 0.0)
        endmembers = jnp.maximum(endmembers - 40.0 * (grad_spectra / pixel_count), 0.0)
    return (current, endmembers)
```

```python
import functools

import jax
import jax.numpy as jnp
from jax import lax
from jax.experimental import pallas as pl
from jax.experimental.pallas import tpu as pltpu
from jax.sharding import PartitionSpec as P

MESH = pl.DeviceIdType.MESH
KS = 9
ITERS = 3
BF = jnp.bfloat16
F32 = jnp.float32
H, W, C = 16, 128, 64
PAIRS = H // 2
EXT = PAIRS + 4
HALF = 216
ROWS = 256


def split(x):
    hi = x.astype(BF)
    return hi, (x - hi.astype(F32)).astype(BF)


def mm(a, b):
    return jnp.dot(a, b, preferred_element_type=F32)


def mm_nt(a, b):
    return lax.dot_general(a, b, (((1,), (1,)), ((), ())), preferred_element_type=F32)


def iota(shape, dim):
    return lax.broadcasted_iota(jnp.int32, shape, dim)


def kernel(
    nr, nc, bands,
    obs_hbm, bend_ref, a_hbm, m_ref, kern_ref, fam_ref,
    out_ref, mout_ref,
    obs_v, a_stage, bend_v, s_main, s_strip, a_main, a_strip, a_hi, a_lo,
    r_up, r_dn, r_one, r_side,
    w_hi, w_lo, wt_hi, wt_lo, fe_hi, fe_lo, as_hi, as_lo,
    bb, g_v, g_hi, g_lo, gc_v, gacc, m_lhs, mt_lhs, q_sel,
    gp, rs_buf, b_src, b_buf, mp,
    in_sem, ex_s, ex_r, rs_s, rs_r, b_s, b_r, c_s, c_r,
):
    r = lax.axis_index("rows")
    c = lax.axis_index("cols")
    has_up, has_dn = r > 0, r < nr - 1
    has_l, has_r = c > 0, c < nc - 1
    rch = ROWS // nc
    npix = float(nr * nc * H * W)

    a_cp = [
        pltpu.make_async_copy(
            a_hbm.at[:, h, :], a_stage.at[h // 2, :, pl.ds((h % 2) * W, W)], in_sem.at[0, h]
        )
        for h in range(H)
    ]
    full = bands // 8 * 8
    tail = bands - full
    o_cp = [
        pltpu.make_async_copy(
            obs_hbm.at[pl.ds(src, size), h, :],
            obs_v.at[h // 2, pl.ds(dst, size), pl.ds((h % 2) * W, W)],
            in_sem.at[k, h],
        )
        for h in range(H)
        for k, src, dst, size in ((1, 0, 0, full), (2, bands - 8, full, 8))
    ]
    for cp in a_cp:
        cp.start()
    for cp in o_cp:
        cp.start()

    barrier = pltpu.get_barrier_semaphore()

    def greet(dr, dc):
        pl.semaphore_signal(barrier, inc=1, device_id=(dr, dc), device_id_type=MESH)

    @pl.loop(1, nc)
    def _(j):
        greet(r, lax.rem(c + j, nc))

    @pl.loop(1, nr)
    def _(j):
        greet(lax.rem(r + j, nr), c)

    corners = (
        (has_up & has_l, -1, -1), (has_up & has_r, -1, 1),
        (has_dn & has_l, 1, -1), (has_dn & has_r, 1, 1),
    )
    for cond, dr, dc in corners:
        @pl.when(cond)
        def _(dr=dr, dc=dc):
            greet(r + dr, c + dc)

    def ex(it):
        up, dn = lax.max(r - 1, 0), lax.min(r + 1, nr - 1)
        lf, rt = lax.max(c - 1, 0), lax.min(c + 1, nc - 1)

        def cp(k, src, dst, dr, dc):
            return pltpu.make_async_remote_copy(
                src_ref=src, dst_ref=dst, send_sem=ex_s.at[it, k], recv_sem=ex_r.at[it, k],
                device_id=(dr, dc), device_id_type=MESH,
            )

        top, bot = s_strip.at[it, 0], s_strip.at[it, 2]
        return (
            (has_dn, has_up, cp(0, s_main.at[it, pl.ds(EXT - 4, 4)], r_up.at[it], dn, c)),
            (has_up, has_dn, cp(1, s_main.at[it, pl.ds(0, 4)], r_dn.at[it], up, c)),
            (has_dn, has_up, cp(2, bot, r_one.at[it, 0], dn, c)),
            (has_up, has_dn, cp(3, top, r_one.at[it, 1], up, c)),
            (has_r, has_l, cp(4, s_strip.at[it], r_side.at[it, 0], r, rt)),
            (has_l, has_r, cp(5, s_strip.at[it], r_side.at[it, 1], r, lf)),
            (has_dn & has_r, has_up & has_l, cp(6, bot, r_one.at[it, 2], dn, rt)),
            (has_dn & has_l, has_up & has_r, cp(7, bot, r_one.at[it, 3], dn, lf)),
            (has_up & has_r, has_dn & has_l, cp(8, top, r_one.at[it, 4], up, rt)),
            (has_up & has_l, has_dn & has_r, cp(9, top, r_one.at[it, 5], up, lf)),
        )

    def ex_start(it):
        for send, _, cp in ex(it):
            @pl.when(send)
            def _(cp=cp):
                cp.start()

    def ex_wait_recv(it):
        for _, recv, cp in ex(it):
            @pl.when(recv)
            def _(cp=cp):
                cp.wait_recv()

    def ex_wait_send(it):
        for send, _, cp in ex(it):
            @pl.when(send)
            def _(cp=cp):
                cp.wait_send()

    @pl.when(jnp.logical_not(has_up))
    def _():
        r_up[...] = jnp.zeros_like(r_up)
        r_one[:, 0] = jnp.zeros((4, C, W), F32)

    @pl.when(jnp.logical_not(has_dn))
    def _():
        r_dn[...] = jnp.zeros_like(r_dn)
        r_one[:, 1] = jnp.zeros((4, C, W), F32)

    @pl.when(jnp.logical_not(has_l))
    def _():
        r_side[:, 0] = jnp.zeros((4, 3, C, W), F32)

    @pl.when(jnp.logical_not(has_r))
    def _():
        r_side[:, 1] = jnp.zeros((4, 3, C, W), F32)

    for k, (cond, _, _) in enumerate(corners):
        @pl.when(jnp.logical_not(cond))
        def _(k=k):
            r_one[:, 2 + k] = jnp.zeros((4, C, W), F32)

    lane = iota((C, W), 1)
    edge_lane = (lane < 4) | (lane >= W - 4)

    zero_pair = jnp.zeros((C, 2 * W), F32)
    for i in (0, 1, EXT - 2, EXT - 1):
        s_main[0, i] = zero_pair
    a_main[...] = jnp.zeros_like(a_main)
    a_strip[...] = jnp.zeros_like(a_strip)
    for cp in a_cp:
        cp.wait()
    for i in range(PAIRS):
        s_main[0, i + 2] = a_stage[i] * (-2.0)
    for t in range(3):
        acc = jnp.zeros((C, W), F32)
        for q in range(8):
            h = 8 * t + q - 4
            if 0 <= h < H:
                row = s_main[0, h // 2 + 2, :, (h % 2) * W:(h % 2 + 1) * W]
                moved = pltpu.roll(row, (16 * q + 8) % W, 1)
                acc = jnp.where((lane >= 16 * q + 4) & (lane < 16 * q + 12), moved, acc)
        s_strip[0, t] = acc

    pl.semaphore_wait(barrier, nc - 1 + nr - 1 + sum(k[0].astype(jnp.int32) for k in corners))
    ex_start(0)

    fam = fam_ref[0, 0]
    row_i, col_i = iota((W, W), 0), iota((W, W), 1)
    zero_blk = jnp.zeros((W, W), BF)
    w_hi[...] = jnp.zeros_like(w_hi)
    w_lo[...] = jnp.zeros_like(w_lo)
    wt_hi[...] = jnp.zeros_like(wt_hi)
    wt_lo[...] = jnp.zeros_like(wt_lo)
    for u in range(KS):
        for diff, hi_ref, lo_ref, flip in (
            (row_i - col_i + 4, w_hi, w_lo, False),
            (col_i - row_i + 4, wt_hi, wt_lo, True),
        ):
            band = jnp.zeros((W, W), F32)
            for v in range(KS):
                band = jnp.where(diff == v, kern_ref[fam, u, v], band)
            hi, lo = split(band)
            for d in range(5):
                for i in range(2):
                    for j in range(2):
                        if 2 * d + i - j == u:
                            a, b = (j, i) if flip else (i, j)
                            sl = (d, pl.ds(a * W, W), pl.ds(b * W, W))
                            hi_ref[sl] = hi
                            lo_ref[sl] = lo

    def table(idx):
        def step(k, acc):
            return jnp.where(idx == k, kern_ref[fam, k // KS, lax.rem(k, KS)], acc)
        return lax.fori_loop(0, KS * KS, step, jnp.zeros((W, W), F32))

    def index(u, v, ok):
        good = ok & (u >= 0) & (u < KS) & (v >= 0) & (v < KS)
        return jnp.where(good, u * KS + v, -1)

    def strip_x(m):
        return jnp.where(m < 4, 128 + m, jnp.where(m < 8, 120 + m, jnp.where(m < 12, m - 8, m - 16)))

    m_row = row_i & 15
    cw = col_i & 7
    w_out = jnp.where(cw < 4, 124 + cw, cw - 4)
    for t in range(3):
        u = 8 * t + (row_i >> 4) - (col_i >> 3)
        v = strip_x(m_row) - w_out + 4
        fe = table(index(u, v, (m_row < 4) | (m_row >= 12)))
        fe_hi[t], fe_lo[t] = split(fe)
    x_in = jnp.where(m_row < 8, 120 + m_row, m_row - 8)
    for t in range(2):
        u = 8 * t + (col_i >> 4) - (row_i >> 4)
        v = strip_x(col_i & 15) - x_in + 4
        as_hi[t], as_lo[t] = split(table(index(u, v, u == u)))

    qr, qc = iota((W, 2 * W), 0), iota((W, 2 * W), 1)
    q_sel[...] = jnp.where(qc == jnp.where(qr < C, qr, qr + C), 1.0, 0.0).astype(BF)
    gacc[...] = jnp.zeros_like(gacc)
    gacc[0:full, 0:C] = m_ref[0:full]
    gacc[2 * HALF - tail:, 0:C] = m_ref[full:bands]
    low = iota((HALF, W), 1) < C
    rows_2 = iota((HALF, W), 0) + HALF
    twice = (rows_2 >= full) & (rows_2 < 2 * HALF - tail)
    md0 = gacc[...] + pltpu.roll(gacc[...], C, 1)
    mp[0, 0:HALF] = jnp.where(low, md0[0:HALF], md0[HALF:])
    mp[0, HALF:ROWS] = jnp.zeros((ROWS - HALF, W), F32)
    gp[:, HALF:ROWS] = jnp.zeros((ITERS, ROWS - HALF, W), F32)
    for h in range(H):
        bend_v[h // 2, :, (h % 2) * W:(h % 2 + 1) * W] = jnp.broadcast_to(
            bend_ref[h:h + 1, :], (8, W)
        )
    g_hi[...] = jnp.zeros_like(g_hi)
    g_lo[...] = jnp.zeros_like(g_lo)

    def spectra_of(k):
        x = mp[k, 0:HALF]
        y = pltpu.roll(x, C, 1)
        return jnp.where(low, x, y), jnp.where(low, y, x)

    def set_spectra(k):
        a, b = spectra_of(k)
        for x, lo_row in ((a, 0), (b, HALF)):
            hi, lo = split(x * (1.0 / C))
            m_lhs[lo_row:lo_row + HALF, 0:W] = hi.astype(F32)
            m_lhs[lo_row:lo_row + HALF, W:] = lo.astype(F32)
        mt_lhs[...] = mm_nt(q_sel[...], m_lhs[...].astype(BF)).astype(BF)

    set_spectra(0)
    for cp in o_cp:
        cp.wait()

    def rs_sum_copies(g):
        whole = rs_buf.at[g, pl.ds(0, nc - 1)]
        return pltpu.make_async_remote_copy(
            src_ref=whole, dst_ref=whole, send_sem=rs_s.at[g], recv_sem=rs_r.at[g],
            device_id=(r, lax.rem(c + 1, nc)), device_id_type=MESH,
        )

    def b_sum_copies(g):
        whole = b_buf.at[g, pl.ds(0, nr - 1)]
        return pltpu.make_async_remote_copy(
            src_ref=whole, dst_ref=whole, send_sem=b_s.at[g], recv_sem=b_r.at[g],
            device_id=(lax.rem(r + 1, nr), c), device_id_type=MESH,
        )

    def c_sum_copies(g):
        whole = mp.at[g + 1, pl.ds(0, ROWS - rch)]
        return pltpu.make_async_remote_copy(
            src_ref=whole, dst_ref=whole, send_sem=c_s.at[g], recv_sem=c_r.at[g],
            device_id=(r, lax.rem(c + 1, nc)), device_id_type=MESH,
        )

    mine = pl.ds(pl.multiple_of(c * rch, rch), rch)

    def rs_start(g):
        rs_buf[g, c] = gp[g, mine]

        @pl.loop(1, nc)
        def _(j):
            t = lax.rem(c + j, nc)
            pltpu.make_async_remote_copy(
                src_ref=gp.at[g, pl.ds(pl.multiple_of(t * rch, rch), rch)],
                dst_ref=rs_buf.at[g, c], send_sem=rs_s.at[g], recv_sem=rs_r.at[g],
                device_id=(r, t), device_id_type=MESH,
            ).start()

    def b_start(g):
        rs_sum_copies(g).wait_recv()
        total = rs_buf[g, 0]
        for j in range(1, nc):
            total = total + rs_buf[g, j]
        b_src[g] = total
        b_buf[g, r] = total

        @pl.loop(1, nr)
        def _(j):
            pltpu.make_async_remote_copy(
                src_ref=b_src.at[g], dst_ref=b_buf.at[g, r],
                send_sem=b_s.at[g], recv_sem=b_r.at[g],
                device_id=(lax.rem(r + j, nr), c), device_id_type=MESH,
            ).start()

    def c_start(g):
        b_sum_copies(g).wait_recv()
        total = b_buf[g, 0]
        for j in range(1, nr):
            total = total + b_buf[g, j]
        mp[g + 1, mine] = jnp.maximum(mp[g, mine] - 40.0 * (total / npix), 0.0)

        @pl.loop(1, nc)
        def _(j):
            pltpu.make_async_remote_copy(
                src_ref=mp.at[g + 1, mine], dst_ref=mp.at[g + 1, mine],
                send_sem=c_s.at[g], recv_sem=c_r.at[g],
                device_id=(r, lax.rem(c + j, nc)), device_id_type=MESH,
            ).start()

    lane_m = lane & 15
    lane_q = lane >> 4

    def update(it):
        xs = []
        for t in range(3):
            left, right = r_side[it, 0, t], r_side[it, 1, t]
            if t == 0:
                left, right = left + r_one[it, 2], right + r_one[it, 3]
            if t == 2:
                left, right = left + r_one[it, 4], right + r_one[it, 5]
            x = jnp.where(lane_m >= 8, pltpu.roll(left, 8, 1), pltpu.roll(right, W - 8, 1))
            xs.append(x)
            total = s_strip[it, t] + x
            ok = ((lane_m < 4) & has_r) | ((lane_m >= 12) & has_l)
            if t == 0:
                total = total + r_one[it, 0]
                ok = ok & ((lane_q >= 4) | has_up)
            if t == 2:
                total = total + r_one[it, 1]
                ok = ok & ((lane_q < 4) | has_dn)
            a_strip[t] = jnp.maximum(a_strip[t] - 0.5 * jnp.where(ok, total, 0.0), 0.0)
        for i in range(EXT):
            for j in range(2):
                e = 2 * i + j
                sl = slice(j * W, (j + 1) * W)
                total = s_main[it, i, :, sl]
                if i < 4:
                    total = total + r_up[it, i, :, sl]
                if i >= EXT - 4:
                    total = total + r_dn[it, i - (EXT - 4), :, sl]
                moved = pltpu.roll(xs[e // 8], (120 - 16 * (e % 8)) % W, 1)
                total = total + jnp.where(edge_lane, moved, 0.0)
                if e < 4:
                    total = jnp.where(has_up, total, 0.0)
                if e >= H + 4:
                    total = jnp.where(has_dn, total, 0.0)
                new = jnp.maximum(a_main[i, :, sl] - 0.5 * total, 0.0)
                a_main[i, :, sl] = new
                hi, lo = split(new)
                a_hi[i, :, sl] = hi
                a_lo[i, :, sl] = lo

    def blur():
        edge = jnp.zeros((C, W), F32)
        for t in range(3):
            hi, lo = split(a_strip[t])
            edge = edge + mm(hi, fe_hi[t]) + mm(lo, fe_hi[t]) + mm(hi, fe_lo[t])
        for half in range(2):
            base = half * 4
            acc = None
            for d in range(5):
                hi = a_hi[base + d:base + d + 4].reshape(4 * C, 2 * W)
                lo = a_lo[base + d:base + d + 4].reshape(4 * C, 2 * W)
                part = mm(hi, w_hi[d]) + mm(lo, w_hi[d]) + mm(hi, w_lo[d])
                acc = part if acc is None else acc + part
            for k in range(4):
                for j in range(2):
                    h = 2 * (base + k) + j
                    moved = pltpu.roll(edge, (-8 * h - 4) % W, 1)
                    val = acc[k * C:(k + 1) * C, j * W:(j + 1) * W]
                    val = val + jnp.where(edge_lane, moved, 0.0)
                    hi, lo = split(val)
                    bb[base + k, 0:C, j * W:(j + 1) * W] = hi
                    bb[base + k, C:, j * W:(j + 1) * W] = lo

    def spectral():
        gacc[...] = jnp.zeros_like(gacc)

        @pl.loop(0, PAIRS)
        def _(p):
            both = bb[p]
            lin = mm(m_lhs[...].astype(BF), jnp.concatenate([both, both], axis=0))
            t = lin * bend_v[p, 0:1, :]
            a = 1.0 + t
            resid = lin * a - obs_v[p]
            hi, lo = split(resid * (a + t))
            gacc[...] += mm_nt(hi, both) + mm_nt(lo, both)
            part = mm(mt_lhs[...], hi) + mm(mt_lhs[...], lo)
            g = part[0:C] + part[C:]
            g_v[p] = g
            ghi, glo = split(g)
            g_hi[p + 4] = ghi
            g_lo[p + 4] = glo

    def pack_grad(it):
        g = gacc[...]
        g = (g + pltpu.roll(g, C, 1)) * (1.0 / C)
        second = jnp.where(twice, 0.0, g[HALF:])
        gp[it, 0:HALF] = jnp.where(low, g[0:HALF], second)

    def adjoint(it):
        for t in range(2):
            acc = jnp.zeros((C, W), F32)
            for q in range(8):
                h = 8 * t + q
                row = g_v[h // 2, :, (h % 2) * W:(h % 2 + 1) * W]
                acc = jnp.where(lane_q == q, pltpu.roll(row, (16 * q + 8) % W, 1), acc)
            gc_v[t] = acc
        h0, l0 = split(gc_v[0])
        h1, l1 = split(gc_v[1])

        def strip(hi, lo, t):
            return mm(hi, as_hi[t]) + mm(lo, as_hi[t]) + mm(hi, as_lo[t])

        s_strip[it, 0] = strip(h0, l0, 0)
        s_strip[it, 1] = strip(h0, l0, 1) + strip(h1, l1, 0)
        s_strip[it, 2] = strip(h1, l1, 1)
        for part in (0, 2, 1):
            base = 4 * part
            acc = None
            for d in range(5):
                if (part == 0 and d == 4) or (part == 2 and d == 0):
                    continue
                lo_row = base - d + 4
                hi = g_hi[lo_row:lo_row + 4].reshape(4 * C, 2 * W)
                lo = g_lo[lo_row:lo_row + 4].reshape(4 * C, 2 * W)
                term = mm(hi, wt_hi[d]) + mm(lo, wt_hi[d]) + mm(hi, wt_lo[d])
                acc = term if acc is None else acc + term
            for k in range(4):
                s_main[it, base + k] = acc[k * C:(k + 1) * C]

    @pl.loop(0, ITERS + 1)
    def _(it):
        @pl.when(it > 0)
        def _():
            b_start(it - 1)

        ex_wait_recv(it)
        update(it)

        @pl.when(it > 0)
        def _():
            c_start(it - 1)

        @pl.when(it < ITERS)
        def _():
            blur()

        @pl.when(it > 0)
        def _():
            c_sum_copies(it - 1).wait_recv()

        @pl.when((it > 0) & (it < ITERS))
        def _():
            set_spectra(it)

        @pl.when(it < ITERS)
        def _():
            spectral()
            pack_grad(it)
            rs_start(it)
            adjoint(it + 1)
            ex_start(it + 1)

        ex_wait_send(it)

        @pl.when(it > 0)
        def _():
            rs_sum_copies(it - 1).wait_send()
            b_sum_copies(it - 1).wait_send()
            c_sum_copies(it - 1).wait_send()

    for h in range(H):
        out_ref[h] = a_main[h // 2 + 2, :, (h % 2) * W:(h % 2 + 1) * W]
    a, b = spectra_of(ITERS)
    mout_ref[0:HALF] = a[:, 0:C]
    mout_ref[HALF:full] = b[0:full - HALF, 0:C]
    mout_ref[full:bands] = b[HALF - tail:, 0:C]


def solution(mesh):
    nr, nc = mesh.shape["rows"], mesh.shape["cols"]
    rch = ROWS // nc

    def on_device(observed, nonlin, abundance, spectra, kernels, tile_family):
        bands = observed.shape[0]
        vm = pltpu.VMEM
        dma = pltpu.SemaphoreType.DMA
        scratch = [
            vm((PAIRS, 2 * HALF, 2 * W), F32), vm((PAIRS, C, 2 * W), F32), vm((PAIRS, 8, 2 * W), F32),
            vm((4, EXT, C, 2 * W), F32), vm((4, 3, C, W), F32),
            vm((EXT, C, 2 * W), F32), vm((3, C, W), F32), vm((EXT, C, 2 * W), BF), vm((EXT, C, 2 * W), BF),
            vm((4, 4, C, 2 * W), F32), vm((4, 4, C, 2 * W), F32), vm((4, 6, C, W), F32),
            vm((4, 2, 3, C, W), F32),
            vm((5, 2 * W, 2 * W), BF), vm((5, 2 * W, 2 * W), BF),
            vm((5, 2 * W, 2 * W), BF), vm((5, 2 * W, 2 * W), BF),
            vm((3, W, W), BF), vm((3, W, W), BF), vm((2, W, W), BF), vm((2, W, W), BF),
            vm((PAIRS, 2 * C, 2 * W), BF), vm((PAIRS, C, 2 * W), F32),
            vm((EXT + 4, C, 2 * W), BF), vm((EXT + 4, C, 2 * W), BF), vm((2, C, W), F32),
            vm((2 * HALF, W), F32), vm((2 * HALF, 2 * W), F32), vm((W, 2 * HALF), BF), vm((W, 2 * W), BF),
            vm((ITERS, ROWS, W), F32), vm((ITERS, nc, rch, W), F32), vm((ITERS, rch, W), F32),
            vm((ITERS, nr, rch, W), F32), vm((ITERS + 1, ROWS, W), F32),
            dma((3, H)), dma((4, 10)), dma((4, 10)),
            dma((ITERS,)), dma((ITERS,)), dma((ITERS,)), dma((ITERS,)), dma((ITERS,)), dma((ITERS,)),
        ]
        any_spec = pl.BlockSpec(memory_space=pl.ANY)
        vspec = pl.BlockSpec(memory_space=pltpu.VMEM)
        sspec = pl.BlockSpec(memory_space=pltpu.SMEM)
        out, m_out = pl.pallas_call(
            functools.partial(kernel, nr, nc, bands),
            out_shape=(
                jax.ShapeDtypeStruct((H, C, W), F32),
                jax.ShapeDtypeStruct((bands, C), F32),
            ),
            in_specs=[any_spec, vspec, any_spec, vspec, sspec, sspec],
            out_specs=(vspec, vspec),
            scratch_shapes=scratch,
            compiler_params=pltpu.CompilerParams(collective_id=0, has_side_effects=True),
            name="unmix",
        )(observed, nonlin, abundance, spectra, kernels, tile_family)
        return jnp.transpose(out, (1, 0, 2)), m_out

    placed = (
        P(None, "rows", "cols"), P("rows", "cols"), P(None, "rows", "cols"),
        P(), P(), P("rows", "cols"),
    )
    return jax.shard_map(
        on_device, mesh=mesh, in_specs=placed,
        out_specs=(P(None, "rows", "cols"), P()), check_vma=False,
    )
```

```python
import functools

import jax
import jax.numpy as jnp
from jax import lax
from jax.experimental import pallas as pl
from jax.experimental.pallas import tpu as pltpu
from jax.sharding import PartitionSpec as P

MESH = pl.DeviceIdType.MESH
KS = 9
ITERS = 3
BF = jnp.bfloat16
F32 = jnp.float32
H, W, C = 16, 128, 64
PAIRS = H // 2
EXT = PAIRS + 4
HALF = 216
ROWS = 256


def split(x):
    hi = x.astype(BF)
    return hi, (x - hi.astype(F32)).astype(BF)


def mm(a, b):
    return jnp.dot(a, b, preferred_element_type=F32)


def mm_nt(a, b):
    return lax.dot_general(a, b, (((1,), (1,)), ((), ())), preferred_element_type=F32)


def iota(shape, dim):
    return lax.broadcasted_iota(jnp.int32, shape, dim)


def kernel(
    nr, nc, bands,
    obs_hbm, bend_ref, a_hbm, m_ref, kern_ref, fam_ref,
    out_hbm, mout_ref,
    obs_v, a_stage, bend_v, s_main, s_strip, a_main, a_strip, a3,
    r_up, r_dn, r_one, r_side, v_buf, x_buf,
    w3, wt3, fe3, as3,
    acc_b, bb, wgt_hi, wgt_lo, g_v, g3, gacc, m_lhs, mt_lhs, q_sel, m_t,
    gp, rs_buf, b_src, b_buf, mp,
    in_sem, ex_s, ex_r, rs_s, rs_r, b_s, b_r, c_s, c_r,
):
    r = lax.axis_index("rows")
    c = lax.axis_index("cols")
    has_up, has_dn = r > 0, r < nr - 1
    has_l, has_r = c > 0, c < nc - 1
    rch = ROWS // nc
    npix = float(nr * nc * H * W)

    barrier = pltpu.get_barrier_semaphore()

    def greet(dr, dc):
        pl.semaphore_signal(barrier, inc=1, device_id=(dr, dc), device_id_type=MESH)

    @pl.loop(1, nc)
    def _(j):
        greet(r, lax.rem(c + j, nc))

    @pl.loop(1, nr)
    def _(j):
        greet(lax.rem(r + j, nr), c)

    a_cp = [
        pltpu.make_async_copy(
            a_hbm.at[:, h, :], a_stage.at[h // 2, :, pl.ds((h % 2) * W, W)], in_sem.at[0, h]
        )
        for h in range(H)
    ]
    full = bands // 8 * 8
    tail = bands - full
    o_cp = [
        pltpu.make_async_copy(
            obs_hbm.at[pl.ds(src, size), h, :],
            obs_v.at[h // 2, pl.ds(dst, size), pl.ds((h % 2) * W, W)],
            in_sem.at[k, h],
        )
        for h in range(H)
        for k, src, dst, size in ((1, 0, 0, full), (2, bands - 8, full, 8))
    ]
    for cp in a_cp:
        cp.start()
    for cp in o_cp:
        cp.start()

    def ex(it):
        up, dn = lax.max(r - 1, 0), lax.min(r + 1, nr - 1)
        lf, rt = lax.max(c - 1, 0), lax.min(c + 1, nc - 1)

        def cp(k, src, dst, dr, dc):
            return pltpu.make_async_remote_copy(
                src_ref=src, dst_ref=dst, send_sem=ex_s.at[it, k], recv_sem=ex_r.at[it, k],
                device_id=(dr, dc), device_id_type=MESH,
            )

        over, halo = it > 0, it < ITERS
        side = (
            (has_r, has_l, cp(4, s_strip.at[it], r_side.at[it, 0], r, rt)),
            (has_l, has_r, cp(5, s_strip.at[it], r_side.at[it, 1], r, lf)),
        )
        rows_a = (
            (has_dn & over, has_up & over,
             cp(0, s_main.at[it, pl.ds(EXT - 2, 2)], r_up.at[it, pl.ds(2, 2)], dn, c)),
            (has_up & over, has_dn & over,
             cp(1, s_main.at[it, pl.ds(0, 2)], r_dn.at[it, pl.ds(0, 2)], up, c)),
        )
        rows_b = (
            (has_dn & halo, has_up & halo,
             cp(6, s_main.at[it, pl.ds(EXT - 4, 2)], r_up.at[it, pl.ds(0, 2)], dn, c)),
            (has_up & halo, has_dn & halo,
             cp(7, s_main.at[it, pl.ds(2, 2)], r_dn.at[it, pl.ds(2, 2)], up, c)),
        )
        ends = (
            (has_dn, has_up, cp(2, v_buf.at[it, 1], r_one.at[it, 0], dn, c)),
            (has_up, has_dn, cp(3, v_buf.at[it, 0], r_one.at[it, 1], up, c)),
        )
        return side, rows_a, rows_b, ends

    def start(copies):
        for send, _, cp in copies:
            @pl.when(send)
            def _(cp=cp):
                cp.start()

    def wait_recv(copies):
        for _, recv, cp in copies:
            @pl.when(recv)
            def _(cp=cp):
                cp.wait_recv()

    def wait_send(copies):
        for send, _, cp in copies:
            @pl.when(send)
            def _(cp=cp):
                cp.wait_send()

    @pl.when(jnp.logical_not(has_up))
    def _():
        r_up[...] = jnp.zeros_like(r_up)
        r_one[:, 0] = jnp.zeros((4, C, W), F32)

    @pl.when(jnp.logical_not(has_dn))
    def _():
        r_dn[...] = jnp.zeros_like(r_dn)
        r_one[:, 1] = jnp.zeros((4, C, W), F32)

    @pl.when(jnp.logical_not(has_l))
    def _():
        r_side[:, 0] = jnp.zeros((4, 3, C, W), F32)

    @pl.when(jnp.logical_not(has_r))
    def _():
        r_side[:, 1] = jnp.zeros((4, 3, C, W), F32)

    @pl.when(has_up)
    def _():
        r_up[0, 2:4] = jnp.zeros((2, C, 2 * W), F32)

    @pl.when(has_dn)
    def _():
        r_dn[0, 0:2] = jnp.zeros((2, C, 2 * W), F32)

    lane = iota((C, W), 1)
    edge_lane = (lane < 4) | (lane >= W - 4)

    zero_pair = jnp.zeros((C, 2 * W), F32)
    for i in (0, 1, EXT - 2, EXT - 1):
        s_main[0, i] = zero_pair
    a_main[...] = jnp.zeros_like(a_main)
    a_strip[...] = jnp.zeros_like(a_strip)
    for cp in a_cp:
        cp.wait()
    for i in range(PAIRS):
        s_main[0, i + 2] = a_stage[i] * (-2.0)
    for t in range(3):
        acc = jnp.zeros((C, W), F32)
        for q in range(8):
            h = 8 * t + q - 4
            if 0 <= h < H:
                row = s_main[0, h // 2 + 2, :, (h % 2) * W:(h % 2 + 1) * W]
                moved = pltpu.roll(row, (16 * q + 8) % W, 1)
                acc = jnp.where((lane >= 16 * q + 4) & (lane < 16 * q + 12), moved, acc)
        s_strip[0, t] = acc

    fam = fam_ref[0, 0]
    row_i, col_i = iota((W, W), 0), iota((W, W), 1)
    for ref in (w3, wt3):
        for d, i, j in ((0, 0, 1), (4, 1, 0)):
            i, j = (j, i) if ref is wt3 else (i, j)
            for k in range(3):
                ref[d, (2 * k + i) * W:(2 * k + i + 1) * W, j * W:(j + 1) * W] = jnp.zeros((W, W), BF)
    for u in range(KS):
        for diff, ref, flip in ((row_i - col_i + 4, w3, False), (col_i - row_i + 4, wt3, True)):
            band = jnp.zeros((W, W), F32)
            for v in range(KS):
                band = jnp.where(diff == v, kern_ref[u, fam, v], band)
            hi, lo = split(band)
            for d in range(5):
                for i in range(2):
                    for j in range(2):
                        if 2 * d + i - j == u:
                            a, b = (j, i) if flip else (i, j)
                            for k, val in ((0, hi), (1, hi), (2, lo)):
                                ref[d, (2 * k + a) * W:(2 * k + a + 1) * W, b * W:(b + 1) * W] = val

    def table(idx):
        def step(u, acc):
            for v in range(KS):
                acc = jnp.where(idx == u * KS + v, kern_ref[u, fam, v], acc)
            return acc
        hi, lo = split(lax.fori_loop(0, KS, step, jnp.zeros((W, W), F32)))
        return jnp.concatenate([hi, hi, lo], axis=0)

    def index(u, v, ok):
        good = ok & (u >= 0) & (u < KS) & (v >= 0) & (v < KS)
        return jnp.where(good, u * KS + v, -1)

    def strip_x(m):
        return jnp.where(m < 4, 128 + m, jnp.where(m < 8, 120 + m, jnp.where(m < 12, m - 8, m - 16)))

    m_row = row_i & 15
    cw = col_i & 7
    w_out = jnp.where(cw < 4, 124 + cw, cw - 4)
    for t in range(3):
        u = 8 * t + (row_i >> 4) - (col_i >> 3)
        v = strip_x(m_row) - w_out + 4
        fe3[t] = table(index(u, v, (m_row < 4) | (m_row >= 12)))
    x_in = jnp.where(m_row < 8, 120 + m_row, m_row - 8)
    for t in range(2):
        u = 8 * t + (col_i >> 4) - (row_i >> 4)
        v = strip_x(col_i & 15) - x_in + 4
        as3[t] = table(index(u, v, u == u))

    pl.semaphore_wait(barrier, nc - 1 + nr - 1)
    for part in ex(0)[:3]:
        start(part)


    qr, qc = iota((W, 2 * W), 0), iota((W, 2 * W), 1)
    q_sel[...] = jnp.where(qc == jnp.where(qr < C, qr, qr + C), 1.0, 0.0).astype(BF)
    m_t[...] = jnp.zeros_like(m_t)
    m_t[0:C, 0:bands] = m_ref[...]
    m_rows = jnp.transpose(m_t[...])
    gacc[0:full] = m_rows[0:full]
    gacc[full:] = jnp.zeros((2 * HALF - full, W), F32)
    gacc[2 * HALF - tail:] = m_rows[full:bands]
    low = iota((HALF, W), 1) < C
    rows_2 = iota((HALF, W), 0) + HALF
    twice = (rows_2 >= full) & (rows_2 < 2 * HALF - tail)
    md0 = gacc[...] + pltpu.roll(gacc[...], C, 1)
    mp[0, 0:HALF] = jnp.where(low, md0[0:HALF], md0[HALF:])
    mp[0, HALF:ROWS] = jnp.zeros((ROWS - HALF, W), F32)
    gp[:, HALF:ROWS] = jnp.zeros((ITERS, ROWS - HALF, W), F32)
    for h in range(H):
        bend_v[h // 2, :, (h % 2) * W:(h % 2 + 1) * W] = jnp.broadcast_to(
            bend_ref[h:h + 1, :], (8, W)
        )

    def spectra_of(k):
        x = mp[k, 0:HALF]
        y = pltpu.roll(x, C, 1)
        return jnp.where(low, x, y), jnp.where(low, y, x)

    def set_spectra(k):
        a, b = spectra_of(k)
        hi, lo = split(jnp.concatenate([a, b], axis=0) * (1.0 / C))
        m_lhs[:, 0:W] = hi
        m_lhs[:, W:] = lo
        mt_lhs[...] = mm_nt(q_sel[...], m_lhs[...]).astype(BF)

    set_spectra(0)
    for cp in o_cp:
        cp.wait()

    def rs_sum_copies(g):
        whole = rs_buf.at[g, pl.ds(0, nc - 1)]
        return pltpu.make_async_remote_copy(
            src_ref=whole, dst_ref=whole, send_sem=rs_s.at[g], recv_sem=rs_r.at[g],
            device_id=(r, lax.rem(c + 1, nc)), device_id_type=MESH,
        )

    def b_sum_copies(g):
        whole = b_buf.at[g, pl.ds(0, nr - 1)]
        return pltpu.make_async_remote_copy(
            src_ref=whole, dst_ref=whole, send_sem=b_s.at[g], recv_sem=b_r.at[g],
            device_id=(lax.rem(r + 1, nr), c), device_id_type=MESH,
        )

    def c_sum_copies(g):
        whole = mp.at[g + 1, pl.ds(0, ROWS - rch)]
        return pltpu.make_async_remote_copy(
            src_ref=whole, dst_ref=whole, send_sem=c_s.at[g], recv_sem=c_r.at[g],
            device_id=(r, lax.rem(c + 1, nc)), device_id_type=MESH,
        )

    mine = pl.ds(pl.multiple_of(c * rch, rch), rch)

    def rs_start(g):
        rs_buf[g, c] = gp[g, mine]

        @pl.loop(1, nc)
        def _(j):
            t = lax.rem(c + j, nc)
            pltpu.make_async_remote_copy(
                src_ref=gp.at[g, pl.ds(pl.multiple_of(t * rch, rch), rch)],
                dst_ref=rs_buf.at[g, c], send_sem=rs_s.at[g], recv_sem=rs_r.at[g],
                device_id=(r, t), device_id_type=MESH,
            ).start()

    def b_start(g):
        rs_sum_copies(g).wait_recv()
        total = rs_buf[g, 0]
        for j in range(1, nc):
            total = total + rs_buf[g, j]
        b_src[g] = total
        b_buf[g, r] = total

        @pl.loop(1, nr)
        def _(j):
            pltpu.make_async_remote_copy(
                src_ref=b_src.at[g], dst_ref=b_buf.at[g, r],
                send_sem=b_s.at[g], recv_sem=b_r.at[g],
                device_id=(lax.rem(r + j, nr), c), device_id_type=MESH,
            ).start()

    def c_start(g):
        b_sum_copies(g).wait_recv()
        total = b_buf[g, 0]
        for j in range(1, nr):
            total = total + b_buf[g, j]
        mp[g + 1, mine] = jnp.maximum(mp[g, mine] - 40.0 * (total / npix), 0.0)

        @pl.loop(1, nc)
        def _(j):
            pltpu.make_async_remote_copy(
                src_ref=mp.at[g + 1, mine], dst_ref=mp.at[g + 1, mine],
                send_sem=c_s.at[g], recv_sem=c_r.at[g],
                device_id=(r, lax.rem(c + j, nc)), device_id_type=MESH,
            ).start()

    lane_m = lane & 15
    lane_q = lane >> 4

    def lhs3(x):
        hi, lo = split(x)
        return jnp.concatenate([hi, lo, hi], axis=1)

    halo_lane = (lane_m < 4) | (lane_m >= 12)

    def sides_in(it):
        for t in range(3):
            left, right = r_side[it, 0, t], r_side[it, 1, t]
            x = jnp.where(lane_m >= 8, pltpu.roll(left, 8, 1), pltpu.roll(right, W - 8, 1))
            x_buf[t] = x
            if t != 1:
                v_buf[it, t // 2] = x + jnp.where(halo_lane, s_strip[it, t], 0.0)

    def update(it, t):
        x = x_buf[t]
        if t != 1:
            x = x + r_one[it, t // 2]
        total = s_strip[it, t] + x
        ok = ((lane_m < 4) & has_r) | ((lane_m >= 12) & has_l)
        if t == 0:
            ok = ok & ((lane_q >= 4) | has_up)
        if t == 2:
            ok = ok & ((lane_q < 4) | has_dn)
        a_strip[t] = jnp.maximum(a_strip[t] - 0.5 * jnp.where(ok, total, 0.0), 0.0)
        for i in range(4 * t, 4 * t + 4):
            for j in range(2):
                e = 2 * i + j
                sl = slice(j * W, (j + 1) * W)
                total = s_main[it, i, :, sl]
                if t == 0:
                    total = total + r_up[it, i, :, sl]
                if t == 2:
                    total = total + r_dn[it, i - (EXT - 4), :, sl]
                moved = pltpu.roll(x, (120 - 16 * (e % 8)) % W, 1)
                total = total + jnp.where(edge_lane, moved, 0.0)
                if e < 4:
                    total = jnp.where(has_up, total, 0.0)
                if e >= H + 4:
                    total = jnp.where(has_dn, total, 0.0)
                new = jnp.maximum(a_main[i, :, sl] - 0.5 * total, 0.0)
                a_main[i, :, sl] = new
                hi, lo = split(new)
                a3[i, :, j * W:(j + 1) * W] = hi
                a3[i, :, (2 + j) * W:(3 + j) * W] = lo
                a3[i, :, (4 + j) * W:(5 + j) * W] = hi

    def blocks(x, n):
        return x.reshape(n, C, 2 * W)

    def blur_inner():
        lhs = a3[4:8].reshape(4 * C, 6 * W)
        acc_b[4:8] = blocks(mm(lhs, w3[0]), 4)
        acc_b[0:4] = blocks(mm(lhs, w3[4]), 4)
        for d in (1, 2, 3):
            acc_b[4 - d:8 - d] += blocks(mm(lhs, w3[d]), 4)

    def blur_outer():
        for d in range(5):
            parts = []
            if d < 4:
                parts.append(a3[d:4].reshape((4 - d) * C, 6 * W))
            if d > 0:
                parts.append(a3[8:8 + d].reshape(d * C, 6 * W))
            res = mm(parts[0] if len(parts) == 1 else jnp.concatenate(parts, axis=0), w3[d])
            if d < 4:
                acc_b[0:4 - d] += blocks(res[0:(4 - d) * C], 4 - d)
            if d > 0:
                acc_b[8 - d:8] += blocks(res[(4 - d) * C:], d)
        edge = mm(lhs3(a_strip[0]), fe3[0]) + mm(lhs3(a_strip[1]), fe3[1]) + mm(lhs3(a_strip[2]), fe3[2])
        for p in range(PAIRS):
            for j in range(2):
                h = 2 * p + j
                moved = pltpu.roll(edge, (-8 * h - 4) % W, 1)
                val = acc_b[p, :, j * W:(j + 1) * W] + jnp.where(edge_lane, moved, 0.0)
                hi, lo = split(val)
                bb[p, 0:C, j * W:(j + 1) * W] = hi
                bb[p, C:, j * W:(j + 1) * W] = lo

    def spectral(it):
        gacc[...] = jnp.zeros_like(gacc)

        @pl.loop(0, PAIRS, unroll=PAIRS)
        def _(p):
            both = bb[p]
            lin = mm(m_lhs[...], jnp.concatenate([both, both], axis=0))
            t = lin * bend_v[p, 0:1, :]
            a = 1.0 + t
            resid = lin * a - obs_v[p]
            hi, lo = split(resid * (a + t))
            wgt_hi[p] = hi
            wgt_lo[p] = lo
            gacc[...] += mm_nt(hi, both) + mm_nt(lo, both)

        g = gacc[...]
        g = (g + pltpu.roll(g, C, 1)) * (1.0 / C)
        second = jnp.where(twice, 0.0, g[HALF:])
        gp[it, 0:HALF] = jnp.where(low, g[0:HALF], second)

    def pixel_grad():
        @pl.loop(0, PAIRS, unroll=PAIRS)
        def _(p):
            part = mm(mt_lhs[...], wgt_hi[p]) + mm(mt_lhs[...], wgt_lo[p])
            g = part[0:C] + part[C:]
            g_v[p] = g
            g3[p] = lhs3(g)

    def adjoint_strips(it):
        packed = []
        for t in range(2):
            acc = jnp.zeros((C, W), F32)
            for q in range(8):
                h = 8 * t + q
                row = g_v[h // 2, :, (h % 2) * W:(h % 2 + 1) * W]
                acc = jnp.where(lane_q == q, pltpu.roll(row, (16 * q + 8) % W, 1), acc)
            packed.append(lhs3(acc))
        s_strip[it, 0] = mm(packed[0], as3[0])
        s_strip[it, 1] = mm(packed[0], as3[1]) + mm(packed[1], as3[0])
        s_strip[it, 2] = mm(packed[1], as3[1])

    def adjoint_outer(it):
        for d in (0, 4, 1, 2, 3):
            parts = []
            if d < 4:
                parts.append(g3[0:4 - d].reshape((4 - d) * C, 6 * W))
            if d > 0:
                parts.append(g3[8 - d:8].reshape(d * C, 6 * W))
            res = mm(parts[0] if len(parts) == 1 else jnp.concatenate(parts, axis=0), wt3[d])
            if d == 0:
                s_main[it, 0:4] = blocks(res, 4)
            elif d == 4:
                s_main[it, 8:12] = blocks(res, 4)
            else:
                s_main[it, d:4] += blocks(res[0:(4 - d) * C], 4 - d)
                s_main[it, 8:8 + d] += blocks(res[(4 - d) * C:], d)

    def adjoint_inner(it):
        for d in range(5):
            res = blocks(mm(g3[4 - d:8 - d].reshape(4 * C, 6 * W), wt3[d]), 4)
            if d == 0:
                s_main[it, 4:8] = res
            else:
                s_main[it, 4:8] += res

    def out_copies():
        return [
            pltpu.make_async_copy(
                a_main.at[h // 2 + 2, :, pl.ds((h % 2) * W, W)], out_hbm.at[:, h, :], in_sem.at[0, h]
            )
            for h in range(H)
        ]

    @pl.loop(0, ITERS + 1)
    def _(it):
        side, rows_a, rows_b, ends = ex(it)
        more = it < ITERS

        @pl.when(it > 0)
        def _():
            b_start(it - 1)

        wait_recv(side)
        sides_in(it)
        start(ends)

        @pl.when(it > 0)
        def _():
            start(rows_b)

        update(it, 1)

        @pl.when(more)
        def _():
            blur_inner()

        @pl.when(it > 0)
        def _():
            c_start(it - 1)

        wait_recv(rows_a)
        wait_recv(rows_b)
        wait_recv(ends)
        update(it, 0)
        update(it, 2)

        @pl.when(more)
        def _():
            blur_outer()

        @pl.when(it == ITERS)
        def _():
            for cp in out_copies():
                cp.start()

        @pl.when(it > 0)
        def _():
            c_sum_copies(it - 1).wait_recv()

        @pl.when((it > 0) & more)
        def _():
            set_spectra(it)

        @pl.when(more)
        def _():
            spectral(it)
            rs_start(it)
            pixel_grad()
            adjoint_strips(it + 1)
            next_side, next_rows, _, _ = ex(it + 1)
            start(next_side)
            adjoint_outer(it + 1)
            start(next_rows)
            adjoint_inner(it + 1)

        wait_send(side)
        wait_send(rows_a)
        wait_send(rows_b)
        wait_send(ends)

        @pl.when(it > 0)
        def _():
            rs_sum_copies(it - 1).wait_send()
            b_sum_copies(it - 1).wait_send()
            c_sum_copies(it - 1).wait_send()

    a, b = spectra_of(ITERS)
    gacc[0:HALF] = a
    gacc[HALF:] = b
    last = gacc[2 * HALF - tail:]
    gacc[full:bands] = last
    m_rows_t = jnp.transpose(jnp.concatenate([gacc[...], jnp.zeros((4 * W - 2 * HALF, W), F32)], axis=0))
    mout_ref[...] = m_rows_t[0:C, 0:bands]
    for cp in out_copies():
        cp.wait()


def solution(mesh):
    nr, nc = mesh.shape["rows"], mesh.shape["cols"]
    rch = ROWS // nc

    def on_device(observed, nonlin, abundance, spectra, kernels, tile_family):
        bands = observed.shape[0]
        vm = pltpu.VMEM
        dma = pltpu.SemaphoreType.DMA
        scratch = [
            vm((PAIRS, 2 * HALF, 2 * W), F32), vm((PAIRS, C, 2 * W), F32), vm((PAIRS, 8, 2 * W), F32),
            vm((4, EXT, C, 2 * W), F32), vm((4, 3, C, W), F32),
            vm((EXT, C, 2 * W), F32), vm((3, C, W), F32), vm((EXT, C, 6 * W), BF),
            vm((4, 4, C, 2 * W), F32), vm((4, 4, C, 2 * W), F32), vm((4, 2, C, W), F32),
            vm((4, 2, 3, C, W), F32), vm((4, 2, C, W), F32), vm((3, C, W), F32),
            vm((5, 6 * W, 2 * W), BF), vm((5, 6 * W, 2 * W), BF),
            vm((3, 3 * W, W), BF), vm((2, 3 * W, W), BF),
            vm((PAIRS, C, 2 * W), F32), vm((PAIRS, 2 * C, 2 * W), BF),
            vm((PAIRS, 2 * HALF, 2 * W), BF), vm((PAIRS, 2 * HALF, 2 * W), BF),
            vm((PAIRS, C, 2 * W), F32), vm((PAIRS, C, 6 * W), BF),
            vm((2 * HALF, W), F32), vm((2 * HALF, 2 * W), BF), vm((W, 2 * HALF), BF), vm((W, 2 * W), BF),
            vm((W, 4 * W), F32),
            vm((ITERS, ROWS, W), F32), vm((ITERS, nc, rch, W), F32), vm((ITERS, rch, W), F32),
            vm((ITERS, nr, rch, W), F32), vm((ITERS + 1, ROWS, W), F32),
            dma((3, H)), dma((4, 8)), dma((4, 8)),
            dma((ITERS,)), dma((ITERS,)), dma((ITERS,)), dma((ITERS,)), dma((ITERS,)), dma((ITERS,)),
        ]
        any_spec = pl.BlockSpec(memory_space=pl.ANY)
        vspec = pl.BlockSpec(memory_space=pltpu.VMEM)
        sspec = pl.BlockSpec(memory_space=pltpu.SMEM)
        out, m_out = pl.pallas_call(
            functools.partial(kernel, nr, nc, bands),
            out_shape=(
                jax.ShapeDtypeStruct(abundance.shape, F32),
                jax.ShapeDtypeStruct((C, bands), F32),
            ),
            in_specs=[any_spec, vspec, any_spec, vspec, sspec, sspec],
            out_specs=(any_spec, vspec),
            scratch_shapes=scratch,
            compiler_params=pltpu.CompilerParams(collective_id=0, has_side_effects=True),
            name="unmix",
        )(observed, nonlin, abundance, spectra.T, jnp.transpose(kernels, (1, 0, 2)), tile_family)
        return out, m_out.T

    placed = (
        P(None, "rows", "cols"), P("rows", "cols"), P(None, "rows", "cols"),
        P(), P(), P("rows", "cols"),
    )
    return jax.shard_map(
        on_device, mesh=mesh, in_specs=placed,
        out_specs=(P(None, "rows", "cols"), P()), check_vma=False,
    )
```

```python
import functools

import jax
import jax.numpy as jnp
from jax import lax
from jax.experimental import pallas as pl
from jax.experimental.pallas import tpu as pltpu
from jax.sharding import PartitionSpec as P

MESH = pl.DeviceIdType.MESH
KS = 9
ITERS = 3
VM_LIMIT = 40 * 1024 * 1024
BF = jnp.bfloat16
F32 = jnp.float32
H, W, C = 16, 128, 64
PAIRS = H // 2
EXT = PAIRS + 4
HALF = 224
BANDS = 432
REST = BANDS - HALF


def split(x):
    hi = x.astype(BF)
    return hi, (x - hi.astype(F32)).astype(BF)


def mm(a, b):
    return jnp.dot(a, b, preferred_element_type=F32)


def mm_nt(a, b):
    return lax.dot_general(a, b, (((1,), (1,)), ((), ())), preferred_element_type=F32)


def iota(shape, dim):
    return lax.broadcasted_iota(jnp.int32, shape, dim)


def chunks(nc):
    rch = (HALF // nc + 7) // 8 * 8
    return rch, HALF // rch


def kernel(
    nr, nc, bands,
    obs_hbm, bend_ref, a_hbm, m_ref, kern_ref, fam_ref,
    a_out, m_out,
    obs_v, a_stage, bend_v, s_main, s_strip, a_main, a_strip, a3,
    r_up, r_dn, r_one, r_side, r_dg, v_buf, x_buf,
    w3, wt3, fe3, as3,
    acc_b, bb, wgt, g_v, g3, gacc, m_lhs, mt_lhs, q_sel, m_t,
    gp, rs_buf, b_src, b_buf, mp,
    in_sem, ex_s, ex_r, dg_s, dg_r, rs_s, rs_r, b_s, b_r, c_s, c_r,
):
    r = lax.axis_index("rows")
    c = lax.axis_index("cols")
    has_up, has_dn = r > 0, r < nr - 1
    has_l, has_r = c > 0, c < nc - 1
    rch, nown = chunks(nc)
    grp = nc // 2
    span = grp * rch
    owner = c < nown
    npix = float(nr * nc * H * W)

    barrier = pltpu.get_barrier_semaphore()

    def greet(dr, dc):
        pl.semaphore_signal(barrier, inc=1, device_id=(dr, dc), device_id_type=MESH)

    @pl.loop(1, nc)
    def _(j):
        greet(r, lax.rem(c + j, nc))

    @pl.loop(1, nr)
    def _(j):
        greet(lax.rem(r + j, nr), c)

    corners = (
        (has_up & has_l, -1, -1), (has_up & has_r, -1, 1),
        (has_dn & has_l, 1, -1), (has_dn & has_r, 1, 1),
    )
    for cond, dr, dc in corners:
        @pl.when(cond)
        def _(dr=dr, dc=dc):
            greet(r + dr, c + dc)

    a_cp = [
        pltpu.make_async_copy(
            a_hbm.at[:, h, :], a_stage.at[h // 2, :, pl.ds((h % 2) * W, W)], in_sem.at[0, h]
        )
        for h in range(H)
    ]
    full = bands // 8 * 8
    tail = bands - full
    o_cp = [
        pltpu.make_async_copy(
            obs_hbm.at[pl.ds(src, size), h, :],
            obs_v.at[h // 2, pl.ds(dst, size), pl.ds((h % 2) * W, W)],
            in_sem.at[k, h],
        )
        for h in range(H)
        for k, src, dst, size in ((1, 0, 0, full), (2, bands - 8, full, 8))
    ]
    for cp in a_cp:
        cp.start()
    for cp in o_cp:
        cp.start()

    def ex(it):
        up, dn = lax.max(r - 1, 0), lax.min(r + 1, nr - 1)
        lf, rt = lax.max(c - 1, 0), lax.min(c + 1, nc - 1)

        def cp(k, src, dst, dr, dc):
            return pltpu.make_async_remote_copy(
                src_ref=src, dst_ref=dst, send_sem=ex_s.at[it, k], recv_sem=ex_r.at[it, k],
                device_id=(dr, dc), device_id_type=MESH,
            )

        over, halo = it > 0, it < ITERS
        side = (
            (has_r, has_l, cp(4, s_strip.at[it], r_side.at[it, 0], r, rt)),
            (has_l, has_r, cp(5, s_strip.at[it], r_side.at[it, 1], r, lf)),
        )
        rows_a = (
            (has_dn & over, has_up & over,
             cp(0, s_main.at[it, pl.ds(EXT - 2, 2)], r_up.at[it, pl.ds(2, 2)], dn, c)),
            (has_up & over, has_dn & over,
             cp(1, s_main.at[it, pl.ds(0, 2)], r_dn.at[it, pl.ds(0, 2)], up, c)),
        )
        rows_b = (
            (has_dn & halo, has_up & halo,
             cp(6, s_main.at[it, pl.ds(EXT - 4, 2)], r_up.at[it, pl.ds(0, 2)], dn, c)),
            (has_up & halo, has_dn & halo,
             cp(7, s_main.at[it, pl.ds(2, 2)], r_dn.at[it, pl.ds(2, 2)], up, c)),
        )
        ends = (
            (has_dn & over, has_up & over, cp(2, v_buf.at[it, 1], r_one.at[it, 0], dn, c)),
            (has_up & over, has_dn & over, cp(3, v_buf.at[it, 0], r_one.at[it, 1], up, c)),
        )
        return side, rows_a, rows_b, ends

    def corner(k, t, dr, dc):
        return pltpu.make_async_remote_copy(
            src_ref=s_strip.at[0, t], dst_ref=r_dg.at[k], send_sem=dg_s.at[k], recv_sem=dg_r.at[k],
            device_id=(lax.clamp(0, r + dr, nr - 1), lax.clamp(0, c + dc, nc - 1)),
            device_id_type=MESH,
        )

    dg = (
        (corners[3][0], corners[0][0], corner(0, 2, 1, 1)),
        (corners[2][0], corners[1][0], corner(1, 2, 1, -1)),
        (corners[1][0], corners[2][0], corner(2, 0, -1, 1)),
        (corners[0][0], corners[3][0], corner(3, 0, -1, -1)),
    )

    def start(copies):
        for send, _, cp in copies:
            @pl.when(send)
            def _(cp=cp):
                cp.start()

    def wait_recv(copies):
        for _, recv, cp in copies:
            @pl.when(recv)
            def _(cp=cp):
                cp.wait_recv()

    def wait_send(copies):
        for send, _, cp in copies:
            @pl.when(send)
            def _(cp=cp):
                cp.wait_send()

    @pl.when(jnp.logical_not(has_up))
    def _():
        r_up[...] = jnp.zeros_like(r_up)
        r_one[:, 0] = jnp.zeros((4, C, W), F32)

    @pl.when(jnp.logical_not(has_dn))
    def _():
        r_dn[...] = jnp.zeros_like(r_dn)
        r_one[:, 1] = jnp.zeros((4, C, W), F32)

    @pl.when(jnp.logical_not(has_l))
    def _():
        r_side[:, 0] = jnp.zeros((4, 3, C, W), F32)

    @pl.when(jnp.logical_not(has_r))
    def _():
        r_side[:, 1] = jnp.zeros((4, 3, C, W), F32)

    @pl.when(has_up)
    def _():
        r_up[0, 2:4] = jnp.zeros((2, C, 2 * W), F32)

    @pl.when(has_dn)
    def _():
        r_dn[0, 0:2] = jnp.zeros((2, C, 2 * W), F32)

    for k, (cond, _, _) in enumerate(corners):
        @pl.when(jnp.logical_not(cond))
        def _(k=k):
            r_dg[k] = jnp.zeros((C, W), F32)

    lane = iota((C, W), 1)
    edge_lane = (lane < 4) | (lane >= W - 4)

    zero_pair = jnp.zeros((C, 2 * W), F32)
    for i in (0, 1, EXT - 2, EXT - 1):
        s_main[0, i] = zero_pair
    a_main[...] = jnp.zeros_like(a_main)
    a_strip[...] = jnp.zeros_like(a_strip)
    for cp in a_cp:
        cp.wait()
    for i in range(PAIRS):
        s_main[0, i + 2] = a_stage[i] * (-2.0)
    for t in range(3):
        acc = jnp.zeros((C, W), F32)
        for q in range(8):
            h = 8 * t + q - 4
            if 0 <= h < H:
                row = s_main[0, h // 2 + 2, :, (h % 2) * W:(h % 2 + 1) * W]
                moved = pltpu.roll(row, (16 * q + 8) % W, 1)
                acc = jnp.where((lane >= 16 * q + 4) & (lane < 16 * q + 12), moved, acc)
        s_strip[0, t] = acc

    fam = fam_ref[0, 0]
    row_i, col_i = iota((W, W), 0), iota((W, W), 1)
    for ref in (w3, wt3):
        for d, i, j in ((0, 0, 1), (4, 1, 0)):
            i, j = (j, i) if ref is wt3 else (i, j)
            for k in range(3):
                ref[d, (2 * k + i) * W:(2 * k + i + 1) * W, j * W:(j + 1) * W] = jnp.zeros((W, W), BF)
    for u in range(KS):
        for diff, ref, flip in ((row_i - col_i + 4, w3, False), (col_i - row_i + 4, wt3, True)):
            band = jnp.zeros((W, W), F32)
            for v in range(KS):
                band = jnp.where(diff == v, kern_ref[u, fam, v], band)
            hi, lo = split(band)
            for d in range(5):
                for i in range(2):
                    for j in range(2):
                        if 2 * d + i - j == u:
                            a, b = (j, i) if flip else (i, j)
                            for k, val in ((0, hi), (1, hi), (2, lo)):
                                ref[d, (2 * k + a) * W:(2 * k + a + 1) * W, b * W:(b + 1) * W] = val

    def table(idx):
        def step(u, acc):
            for v in range(KS):
                acc = jnp.where(idx == u * KS + v, kern_ref[u, fam, v], acc)
            return acc
        hi, lo = split(lax.fori_loop(0, KS, step, jnp.zeros((W, W), F32)))
        return jnp.concatenate([hi, hi, lo], axis=0)

    def index(u, v, ok):
        good = ok & (u >= 0) & (u < KS) & (v >= 0) & (v < KS)
        return jnp.where(good, u * KS + v, -1)

    def strip_x(m):
        return jnp.where(m < 4, 128 + m, jnp.where(m < 8, 120 + m, jnp.where(m < 12, m - 8, m - 16)))

    m_row = row_i & 15
    cw = col_i & 7
    w_out = jnp.where(cw < 4, 124 + cw, cw - 4)
    for t in range(3):
        u = 8 * t + (row_i >> 4) - (col_i >> 3)
        v = strip_x(m_row) - w_out + 4
        fe3[t] = table(index(u, v, (m_row < 4) | (m_row >= 12)))
    x_in = jnp.where(m_row < 8, 120 + m_row, m_row - 8)
    for t in range(2):
        u = 8 * t + (col_i >> 4) - (row_i >> 4)
        v = strip_x(col_i & 15) - x_in + 4
        as3[t] = table(index(u, v, u == u))

    pl.semaphore_wait(barrier, nc - 1 + nr - 1 + sum(k[0].astype(jnp.int32) for k in corners))
    start(dg)
    first_side, _, first_rows, _ = ex(0)
    start(first_side)
    start(first_rows)


    qr, qc = iota((W, 2 * W), 0), iota((W, 2 * W), 1)
    q_sel[...] = jnp.where(qc == jnp.where(qr < C, qr, qr + C), 1.0, 0.0).astype(BF)
    m_t[...] = jnp.zeros_like(m_t)
    m_t[0:C, 0:bands] = m_ref[...]
    m_rows = jnp.transpose(m_t[...])
    gacc[0:full] = m_rows[0:full]
    gacc[full:] = jnp.zeros((BANDS - full, W), F32)
    gacc[BANDS - tail:] = m_rows[full:bands]
    low = iota((HALF, W), 1) < C
    md0 = gacc[...] + pltpu.roll(gacc[...], C, 1)
    blank = jnp.zeros((HALF - REST, W), F32)
    mp[0] = jnp.where(low, md0[0:HALF], jnp.concatenate([md0[HALF:], blank], axis=0))
    wgt[BANDS:] = jnp.zeros((HALF + 2 * span - BANDS, 2 * PAIRS * 2 * W), BF)
    for h in range(H):
        bend_v[h // 2, :, (h % 2) * W:(h % 2 + 1) * W] = jnp.broadcast_to(
            bend_ref[h:h + 1, :], (8, W)
        )

    def spectra_of(k):
        x = mp[k]
        y = pltpu.roll(x, C, 1)
        return jnp.concatenate([jnp.where(low, x, y), jnp.where(low, y, x)[0:REST]], axis=0)

    def set_spectra(k):
        hi, lo = split(spectra_of(k) * (1.0 / C))
        m_lhs[:, 0:W] = hi
        m_lhs[:, W:] = lo

    def set_transposed():
        mt_lhs[...] = mm_nt(q_sel[...], m_lhs[...]).astype(BF)

    for cp in o_cp:
        cp.wait()

    def many(ref, n, g, s_sem, r_sem, dr, dc):
        whole = ref.at[g, pl.ds(0, n)]
        return pltpu.make_async_remote_copy(
            src_ref=whole, dst_ref=whole, send_sem=s_sem.at[g], recv_sem=r_sem.at[g],
            device_id=(dr, dc), device_id_type=MESH,
        )

    next_c, next_r = lax.rem(c + 1, nc), lax.rem(r + 1, nr)

    def rs_many(n, g):
        return many(rs_buf, n, g, rs_s, rs_r, r, next_c)

    def b_many(g):
        return many(b_buf, nr - 1, g, b_s, b_r, next_r, c)

    def c_many(rows, g):
        whole = mp.at[g + 1, pl.ds(0, rows)]
        return pltpu.make_async_remote_copy(
            src_ref=whole, dst_ref=whole, send_sem=c_s.at[g], recv_sem=c_r.at[g],
            device_id=(r, next_c), device_id_type=MESH,
        )

    def chunk(k):
        return pl.ds(pl.multiple_of(k * rch, rch), rch)

    def rs_start(g, half):
        @pl.loop(0, grp)
        def _(j):
            k = half * grp + j

            @pl.when((k < nown) & (k != c))
            def _():
                pltpu.make_async_remote_copy(
                    src_ref=gp.at[g, chunk(k)], dst_ref=rs_buf.at[g, c],
                    send_sem=rs_s.at[g], recv_sem=rs_r.at[g],
                    device_id=(r, k), device_id_type=MESH,
                ).start()

    def b_start(g):
        @pl.when(owner)
        def _():
            rs_buf[g, c] = gp[g, chunk(c)]
            rs_many(nc - 1, g).wait_recv()
            total = rs_buf[g, 0]
            for j in range(1, nc):
                total = total + rs_buf[g, j]
            b_src[g] = total
            b_buf[g, r] = total

            @pl.loop(1, nr)
            def _(j):
                pltpu.make_async_remote_copy(
                    src_ref=b_src.at[g], dst_ref=b_buf.at[g, r],
                    send_sem=b_s.at[g], recv_sem=b_r.at[g],
                    device_id=(lax.rem(r + j, nr), c), device_id_type=MESH,
                ).start()

    def c_start(g):
        @pl.when(owner)
        def _():
            b_many(g).wait_recv()
            total = b_buf[g, 0]
            for j in range(1, nr):
                total = total + b_buf[g, j]
            mine = chunk(c)
            mp[g + 1, mine] = jnp.maximum(mp[g, mine] - 40.0 * (total / npix), 0.0)

            @pl.loop(1, nc)
            def _(j):
                pltpu.make_async_remote_copy(
                    src_ref=mp.at[g + 1, mine], dst_ref=mp.at[g + 1, mine],
                    send_sem=c_s.at[g], recv_sem=c_r.at[g],
                    device_id=(r, lax.rem(c + j, nc)), device_id_type=MESH,
                ).start()

    def c_wait(g):
        @pl.when(owner)
        def _():
            c_many((nown - 1) * rch, g).wait_recv()

        @pl.when(jnp.logical_not(owner))
        def _():
            c_many(nown * rch, g).wait_recv()

    def sent(g):
        @pl.when(owner)
        def _():
            rs_many(nown - 1, g).wait_send()
            b_many(g).wait_send()
            many(rs_buf, nc - 1, g, c_s, c_r, r, next_c).wait_send()

        @pl.when(jnp.logical_not(owner))
        def _():
            rs_many(nown, g).wait_send()

    lane_m = lane & 15
    lane_q = lane >> 4

    def lhs3(x):
        hi, lo = split(x)
        return jnp.concatenate([hi, lo, hi], axis=1)

    halo_lane = (lane_m < 4) | (lane_m >= 12)

    def sides_in(it):
        for t in range(3):
            left, right = r_side[it, 0, t], r_side[it, 1, t]
            x = jnp.where(lane_m >= 8, pltpu.roll(left, 8, 1), pltpu.roll(right, W - 8, 1))
            x_buf[t] = x
            if t != 1:
                v_buf[it, t // 2] = x + jnp.where(halo_lane, s_strip[it, t], 0.0)

    def update(it, t):
        x = x_buf[t]
        if t != 1:
            x = x + r_one[it, t // 2]
        total = s_strip[it, t] + x
        ok = ((lane_m < 4) & has_r) | ((lane_m >= 12) & has_l)
        if t == 0:
            ok = ok & ((lane_q >= 4) | has_up)
        if t == 2:
            ok = ok & ((lane_q < 4) | has_dn)
        a_strip[t] = jnp.maximum(a_strip[t] - 0.5 * jnp.where(ok, total, 0.0), 0.0)
        for i in range(4 * t, 4 * t + 4):
            for j in range(2):
                e = 2 * i + j
                sl = slice(j * W, (j + 1) * W)
                total = s_main[it, i, :, sl]
                if t == 0:
                    total = total + r_up[it, i, :, sl]
                if t == 2:
                    total = total + r_dn[it, i - (EXT - 4), :, sl]
                moved = pltpu.roll(x, (120 - 16 * (e % 8)) % W, 1)
                total = total + jnp.where(edge_lane, moved, 0.0)
                if e < 4:
                    total = jnp.where(has_up, total, 0.0)
                if e >= H + 4:
                    total = jnp.where(has_dn, total, 0.0)
                new = jnp.maximum(a_main[i, :, sl] - 0.5 * total, 0.0)
                a_main[i, :, sl] = new
                hi, lo = split(new)
                a3[i, :, j * W:(j + 1) * W] = hi
                a3[i, :, (2 + j) * W:(3 + j) * W] = lo
                a3[i, :, (4 + j) * W:(5 + j) * W] = hi

    def blocks(x, n):
        return x.reshape(n, C, 2 * W)

    def blur_inner():
        lhs = a3[4:8].reshape(4 * C, 6 * W)
        acc_b[4:8] = blocks(mm(lhs, w3[0]), 4)
        acc_b[0:4] = blocks(mm(lhs, w3[4]), 4)
        for d in (1, 2, 3):
            acc_b[4 - d:8 - d] += blocks(mm(lhs, w3[d]), 4)

    def blur_outer():
        for d in range(5):
            parts = []
            if d < 4:
                parts.append(a3[d:4].reshape((4 - d) * C, 6 * W))
            if d > 0:
                parts.append(a3[8:8 + d].reshape(d * C, 6 * W))
            res = mm(parts[0] if len(parts) == 1 else jnp.concatenate(parts, axis=0), w3[d])
            if d < 4:
                acc_b[0:4 - d] += blocks(res[0:(4 - d) * C], 4 - d)
            if d > 0:
                acc_b[8 - d:8] += blocks(res[(4 - d) * C:], d)
        edge = mm(lhs3(a_strip[0]), fe3[0]) + mm(lhs3(a_strip[1]), fe3[1]) + mm(lhs3(a_strip[2]), fe3[2])
        for p in range(PAIRS):
            for j in range(2):
                h = 2 * p + j
                moved = pltpu.roll(edge, (-8 * h - 4) % W, 1)
                val = acc_b[p, :, j * W:(j + 1) * W] + jnp.where(edge_lane, moved, 0.0)
                hi, lo = split(val)
                bb[0:C, h * W:(h + 1) * W] = hi
                bb[C:, h * W:(h + 1) * W] = lo

    def pair(p, k=0):
        lo = (k * PAIRS + p) * 2 * W
        return slice(lo, lo + 2 * W)

    def spectral():
        for p in range(PAIRS):
            both = bb[:, pair(p)]
            lin = mm(m_lhs[...], jnp.concatenate([both, both], axis=0))
            t = lin * bend_v[p, 0:1, :]
            a = 1.0 + t
            resid = lin * a - obs_v[p]
            hi, lo = split(resid * (a + t))
            wgt[0:BANDS, pair(p)] = hi
            wgt[0:BANDS, pair(p, 1)] = lo

    low_span = iota((span, W), 1) < C
    span_row = iota((span, W), 0)

    def spectra_grad(it, half):
        parts = []
        for first in (0, HALF):
            rows = pl.ds(pl.multiple_of(first + half * span, 16), span)
            g = mm_nt(wgt[rows, 0:PAIRS * 2 * W], bb[...]) + mm_nt(wgt[rows, PAIRS * 2 * W:], bb[...])
            parts.append((g + pltpu.roll(g, C, 1)) * (1.0 / C))
        row = span_row + (half * span + HALF)
        second = jnp.where((row >= full) & (row < BANDS - tail), 0.0, parts[1])
        gp[it, pl.ds(pl.multiple_of(half * span, 8), span)] = jnp.where(low_span, parts[0], second)

    def pixel_grad():
        for p in range(PAIRS):
            part = mm(mt_lhs[...], wgt[0:BANDS, pair(p)]) + mm(mt_lhs[...], wgt[0:BANDS, pair(p, 1)])
            g = part[0:C] + part[C:]
            g_v[p] = g
            g3[p] = lhs3(g)

    def adjoint_strips(it):
        packed = []
        for t in range(2):
            acc = jnp.zeros((C, W), F32)
            for q in range(8):
                h = 8 * t + q
                row = g_v[h // 2, :, (h % 2) * W:(h % 2 + 1) * W]
                acc = jnp.where(lane_q == q, pltpu.roll(row, (16 * q + 8) % W, 1), acc)
            packed.append(lhs3(acc))
        s_strip[it, 0] = mm(packed[0], as3[0])
        s_strip[it, 1] = mm(packed[0], as3[1]) + mm(packed[1], as3[0])
        s_strip[it, 2] = mm(packed[1], as3[1])

    def adjoint_outer(it):
        for d in (0, 4, 1, 2, 3):
            parts = []
            if d < 4:
                parts.append(g3[0:4 - d].reshape((4 - d) * C, 6 * W))
            if d > 0:
                parts.append(g3[8 - d:8].reshape(d * C, 6 * W))
            res = mm(parts[0] if len(parts) == 1 else jnp.concatenate(parts, axis=0), wt3[d])
            if d == 0:
                s_main[it, 0:4] = blocks(res, 4)
            elif d == 4:
                s_main[it, 8:12] = blocks(res, 4)
            else:
                s_main[it, d:4] += blocks(res[0:(4 - d) * C], 4 - d)
                s_main[it, 8:8 + d] += blocks(res[(4 - d) * C:], d)

    def adjoint_inner(it):
        for d in range(5):
            res = blocks(mm(g3[4 - d:8 - d].reshape(4 * C, 6 * W), wt3[d]), 4)
            if d == 0:
                s_main[it, 4:8] = res
            else:
                s_main[it, 4:8] += res

    mine_half = c // grp

    @pl.loop(0, ITERS + 1)
    def _(it):
        side, rows_a, rows_b, ends = ex(it)
        more = it < ITERS

        @pl.when(it > 0)
        def _():
            b_start(it - 1)

        wait_recv(side)
        sides_in(it)
        start(ends)

        @pl.when(it > 0)
        def _():
            start(rows_b)

        update(it, 1)

        @pl.when(more)
        def _():
            blur_inner()

        @pl.when(it > 0)
        def _():
            c_start(it - 1)

        @pl.when(it == 0)
        def _():
            wait_recv(dg)
            for k in range(2):
                left, right = r_dg[2 * k], r_dg[2 * k + 1]
                r_one[0, k] = jnp.where(
                    lane_m >= 8, pltpu.roll(left, 8, 1), pltpu.roll(right, W - 8, 1)
                )

        wait_recv(ends)
        wait_recv(rows_a)
        wait_recv(rows_b)
        update(it, 0)
        update(it, 2)

        @pl.when(more)
        def _():
            blur_outer()

        @pl.when(jnp.logical_not(more))
        def _():
            a_out[...] = a_main[2:EXT - 2]

        @pl.when(it > 0)
        def _():
            c_wait(it - 1)

        @pl.when(more)
        def _():
            set_spectra(it)
            spectral()
            spectra_grad(it, 1 - mine_half)
            rs_start(it, 1 - mine_half)
            spectra_grad(it, mine_half)
            rs_start(it, mine_half)
            set_transposed()
            pixel_grad()
            adjoint_strips(it + 1)
            next_side, next_rows, _, _ = ex(it + 1)
            start(next_side)
            adjoint_outer(it + 1)
            start(next_rows)
            adjoint_inner(it + 1)

        wait_send(side)
        wait_send(rows_a)
        wait_send(rows_b)
        wait_send(ends)

        @pl.when(it > 0)
        def _():
            sent(it - 1)

    wait_send(dg)
    m_out[...] = mp[ITERS]


def finish(bands, a_ref, m_ref, a_hbm, mt_ref, m_v, sem):
    copies = [
        pltpu.make_async_copy(
            a_ref.at[h // 2, :, pl.ds((h % 2) * W, W)], a_hbm.at[:, h, :], sem.at[h]
        )
        for h in range(H)
    ]
    for cp in copies:
        cp.start()
    full = bands // 8 * 8
    tail = bands - full
    m_v[...] = jnp.zeros_like(m_v)
    m_v[0:HALF] = m_ref[...]
    m_v[HALF:BANDS] = pltpu.roll(m_ref[0:REST], C, 1)
    last = m_v[BANDS - tail:BANDS]
    m_v[full:bands] = last
    mt_ref[...] = jnp.transpose(m_v[...])[0:C, 0:bands]
    for cp in copies:
        cp.wait()


def solution(mesh):
    nr, nc = mesh.shape["rows"], mesh.shape["cols"]
    rch, _ = chunks(nc)

    def on_device(observed, nonlin, abundance, spectra, kernels, tile_family):
        bands = observed.shape[0]
        vm = pltpu.VMEM
        dma = pltpu.SemaphoreType.DMA
        scratch = [
            vm((PAIRS, BANDS, 2 * W), F32), vm((PAIRS, C, 2 * W), F32), vm((PAIRS, 8, 2 * W), F32),
            vm((4, EXT, C, 2 * W), F32), vm((4, 3, C, W), F32),
            vm((EXT, C, 2 * W), F32), vm((3, C, W), F32), vm((EXT, C, 6 * W), BF),
            vm((4, 4, C, 2 * W), F32), vm((4, 4, C, 2 * W), F32), vm((4, 2, C, W), F32),
            vm((4, 2, 3, C, W), F32), vm((4, C, W), F32), vm((4, 2, C, W), F32), vm((3, C, W), F32),
            vm((5, 6 * W, 2 * W), BF), vm((5, 6 * W, 2 * W), BF),
            vm((3, 3 * W, W), BF), vm((2, 3 * W, W), BF),
            vm((PAIRS, C, 2 * W), F32), vm((2 * C, PAIRS * 2 * W), BF),
            vm((HALF + nc // 2 * rch * 2, 2 * PAIRS * 2 * W), BF),
            vm((PAIRS, C, 2 * W), F32), vm((PAIRS, C, 6 * W), BF),
            vm((BANDS, W), F32), vm((BANDS, 2 * W), BF), vm((W, BANDS), BF), vm((W, 2 * W), BF),
            vm((W, 4 * W), F32),
            vm((ITERS, nc // 2 * rch * 2, W), F32), vm((ITERS, nc, rch, W), F32), vm((ITERS, rch, W), F32),
            vm((ITERS, nr, rch, W), F32), vm((ITERS + 1, HALF, W), F32),
            dma((3, H)), dma((4, 8)), dma((4, 8)), dma((4,)), dma((4,)),
            dma((ITERS,)), dma((ITERS,)), dma((ITERS,)), dma((ITERS,)), dma((ITERS,)), dma((ITERS,)),
        ]
        def held(x):
            return pltpu.with_memory_space_constraint(x, pltpu.HBM)

        any_spec = pl.BlockSpec(memory_space=pltpu.HBM)
        vspec = pl.BlockSpec(memory_space=pltpu.VMEM)
        sspec = pl.BlockSpec(memory_space=pltpu.SMEM)
        out, m_out = pl.pallas_call(
            functools.partial(kernel, nr, nc, bands),
            out_shape=(
                jax.ShapeDtypeStruct((PAIRS, C, 2 * W), F32),
                jax.ShapeDtypeStruct((HALF, W), F32),
            ),
            in_specs=[any_spec, vspec, any_spec, vspec, sspec, sspec],
            out_specs=(vspec, vspec),
            scratch_shapes=scratch,
            compiler_params=pltpu.CompilerParams(collective_id=0, has_side_effects=True, vmem_limit_bytes=VM_LIMIT),
            name="unmix",
        )(held(observed), held(nonlin), held(abundance), held(spectra.T), held(jnp.transpose(kernels, (1, 0, 2))), tile_family)
        out, m_out = pl.pallas_call(
            functools.partial(finish, bands),
            out_shape=(
                jax.ShapeDtypeStruct(abundance.shape, F32),
                jax.ShapeDtypeStruct((C, bands), F32),
            ),
            in_specs=[vspec, vspec],
            out_specs=(pl.BlockSpec(memory_space=pltpu.HBM), vspec),
            scratch_shapes=[vm((4 * W, W), F32), dma((H,))],
            compiler_params=pltpu.CompilerParams(vmem_limit_bytes=8 * 1024 * 1024),
            name="finish",
        )(out, m_out)
        return out, m_out.T

    placed = (
        P(None, "rows", "cols"), P("rows", "cols"), P(None, "rows", "cols"),
        P(), P(), P("rows", "cols"),
    )
    return jax.shard_map(
        on_device, mesh=mesh, in_specs=placed,
        out_specs=(P(None, "rows", "cols"), P()), check_vma=False,
    )
```

```python
import functools

import jax
import jax.numpy as jnp
from jax import lax
from jax.experimental import pallas as pl
from jax.experimental.pallas import tpu as pltpu
from jax.sharding import PartitionSpec as P

MESH = pl.DeviceIdType.MESH
KS = 9
ITERS = 3
VM_LIMIT = 40 * 1024 * 1024
BF = jnp.bfloat16
F32 = jnp.float32
H, W, C = 16, 128, 64
PAIRS = H // 2
EXT = PAIRS + 4
HALF = 224
BANDS = 432
REST = BANDS - HALF


def split(x):
    hi = x.astype(BF)
    return hi, (x - hi.astype(F32)).astype(BF)


def mm(a, b):
    return jnp.dot(a, b, preferred_element_type=F32)


def mm_nt(a, b):
    return lax.dot_general(a, b, (((1,), (1,)), ((), ())), preferred_element_type=F32)


def iota(shape, dim):
    return lax.broadcasted_iota(jnp.int32, shape, dim)


def chunks(nc):
    rch = (HALF // nc + 7) // 8 * 8
    return rch, HALF // rch


def kernel(
    nr, nc, bands,
    obs_hbm, bend_ref, a_hbm, m_ref, kern_ref, fam_ref,
    a_out, m_out,
    obs_v, a_stage, bend_v, s_main, s_strip, a_main, a_strip, a3,
    r_up, r_dn, r_one, r_side, r_dg, v_buf, x_buf,
    w3, wt3, fe3, as3,
    acc_b, bb, wgt, g_v, g3, gacc, m_lhs, mt_lhs, q_sel, m_t,
    gp, rs_buf, b_src, b_buf, mp,
    in_sem, ex_s, ex_r, dg_s, dg_r, rs_s, rs_r, b_s, b_r, c_s, c_r,
):
    r = lax.axis_index("rows")
    c = lax.axis_index("cols")
    has_up, has_dn = r > 0, r < nr - 1
    has_l, has_r = c > 0, c < nc - 1
    rch, nown = chunks(nc)
    grp = nc // 2
    span = grp * rch
    owner = c < nown
    npix = float(nr * nc * H * W)

    barrier = pltpu.get_barrier_semaphore()

    def greet(dr, dc):
        pl.semaphore_signal(barrier, inc=1, device_id=(dr, dc), device_id_type=MESH)

    @pl.loop(1, nc)
    def _(j):
        greet(r, lax.rem(c + j, nc))

    @pl.loop(1, nr)
    def _(j):
        greet(lax.rem(r + j, nr), c)

    corners = (
        (has_up & has_l, -1, -1), (has_up & has_r, -1, 1),
        (has_dn & has_l, 1, -1), (has_dn & has_r, 1, 1),
    )
    for cond, dr, dc in corners:
        @pl.when(cond)
        def _(dr=dr, dc=dc):
            greet(r + dr, c + dc)

    a_cp = [
        pltpu.make_async_copy(
            a_hbm.at[:, h, :], a_stage.at[h // 2, :, pl.ds((h % 2) * W, W)], in_sem.at[0, h]
        )
        for h in range(H)
    ]
    full = bands // 8 * 8
    tail = bands - full
    o_cp = [
        pltpu.make_async_copy(
            obs_hbm.at[pl.ds(src, size), h, :],
            obs_v.at[h // 2, pl.ds(dst, size), pl.ds((h % 2) * W, W)],
            in_sem.at[k, h],
        )
        for h in range(H)
        for k, src, dst, size in ((1, 0, 0, full), (2, bands - 8, full, 8))
    ]
    for cp in a_cp:
        cp.start()
    for cp in o_cp:
        cp.start()

    def ex(it):
        up, dn = lax.max(r - 1, 0), lax.min(r + 1, nr - 1)
        lf, rt = lax.max(c - 1, 0), lax.min(c + 1, nc - 1)

        def cp(k, src, dst, dr, dc):
            return pltpu.make_async_remote_copy(
                src_ref=src, dst_ref=dst, send_sem=ex_s.at[it, k], recv_sem=ex_r.at[it, k],
                device_id=(dr, dc), device_id_type=MESH,
            )

        over, halo = it > 0, it < ITERS
        side = (
            (has_r, has_l, cp(4, s_strip.at[it], r_side.at[it, 0], r, rt)),
            (has_l, has_r, cp(5, s_strip.at[it], r_side.at[it, 1], r, lf)),
        )
        rows_a = (
            (has_dn & over, has_up & over,
             cp(0, s_main.at[it, pl.ds(EXT - 2, 2)], r_up.at[it, pl.ds(2, 2)], dn, c)),
            (has_up & over, has_dn & over,
             cp(1, s_main.at[it, pl.ds(0, 2)], r_dn.at[it, pl.ds(0, 2)], up, c)),
        )
        rows_b = (
            (has_dn & halo, has_up & halo,
             cp(6, s_main.at[it, pl.ds(EXT - 4, 2)], r_up.at[it, pl.ds(0, 2)], dn, c)),
            (has_up & halo, has_dn & halo,
             cp(7, s_main.at[it, pl.ds(2, 2)], r_dn.at[it, pl.ds(2, 2)], up, c)),
        )
        ends = (
            (has_dn & over, has_up & over, cp(2, v_buf.at[it, 1], r_one.at[it, 0], dn, c)),
            (has_up & over, has_dn & over, cp(3, v_buf.at[it, 0], r_one.at[it, 1], up, c)),
        )
        return side, rows_a, rows_b, ends

    def corner(k, t, dr, dc):
        return pltpu.make_async_remote_copy(
            src_ref=s_strip.at[0, t], dst_ref=r_dg.at[k], send_sem=dg_s.at[k], recv_sem=dg_r.at[k],
            device_id=(lax.clamp(0, r + dr, nr - 1), lax.clamp(0, c + dc, nc - 1)),
            device_id_type=MESH,
        )

    dg = (
        (corners[3][0], corners[0][0], corner(0, 2, 1, 1)),
        (corners[2][0], corners[1][0], corner(1, 2, 1, -1)),
        (corners[1][0], corners[2][0], corner(2, 0, -1, 1)),
        (corners[0][0], corners[3][0], corner(3, 0, -1, -1)),
    )

    def start(copies):
        for send, _, cp in copies:
            @pl.when(send)
            def _(cp=cp):
                cp.start()

    def wait_recv(copies):
        for _, recv, cp in copies:
            @pl.when(recv)
            def _(cp=cp):
                cp.wait_recv()

    def wait_send(copies):
        for send, _, cp in copies:
            @pl.when(send)
            def _(cp=cp):
                cp.wait_send()

    @pl.when(jnp.logical_not(has_up))
    def _():
        r_up[...] = jnp.zeros_like(r_up)
        r_one[:, 0] = jnp.zeros((4, C, W), F32)

    @pl.when(jnp.logical_not(has_dn))
    def _():
        r_dn[...] = jnp.zeros_like(r_dn)
        r_one[:, 1] = jnp.zeros((4, C, W), F32)

    @pl.when(jnp.logical_not(has_l))
    def _():
        r_side[:, 0] = jnp.zeros((4, 3, C, W), F32)

    @pl.when(jnp.logical_not(has_r))
    def _():
        r_side[:, 1] = jnp.zeros((4, 3, C, W), F32)

    @pl.when(has_up)
    def _():
        r_up[0, 2:4] = jnp.zeros((2, C, 2 * W), F32)

    @pl.when(has_dn)
    def _():
        r_dn[0, 0:2] = jnp.zeros((2, C, 2 * W), F32)

    for k, (cond, _, _) in enumerate(corners):
        @pl.when(jnp.logical_not(cond))
        def _(k=k):
            r_dg[k] = jnp.zeros((C, W), F32)

    lane = iota((C, W), 1)
    edge_lane = (lane < 4) | (lane >= W - 4)

    zero_pair = jnp.zeros((C, 2 * W), F32)
    for i in (0, 1, EXT - 2, EXT - 1):
        s_main[0, i] = zero_pair
    a_main[...] = jnp.zeros_like(a_main)
    a_strip[...] = jnp.zeros_like(a_strip)
    for cp in a_cp:
        cp.wait()
    for i in range(PAIRS):
        s_main[0, i + 2] = a_stage[i] * (-2.0)
    for t in range(3):
        acc = jnp.zeros((C, W), F32)
        for q in range(8):
            h = 8 * t + q - 4
            if 0 <= h < H:
                row = s_main[0, h // 2 + 2, :, (h % 2) * W:(h % 2 + 1) * W]
                moved = pltpu.roll(row, (16 * q + 8) % W, 1)
                acc = jnp.where((lane >= 16 * q + 4) & (lane < 16 * q + 12), moved, acc)
        s_strip[0, t] = acc

    fam = fam_ref[0, 0]
    row_i, col_i = iota((W, W), 0), iota((W, W), 1)
    for ref in (w3, wt3):
        for d, i, j in ((0, 0, 1), (4, 1, 0)):
            i, j = (j, i) if ref is wt3 else (i, j)
            for k in range(3):
                ref[d, (2 * k + i) * W:(2 * k + i + 1) * W, j * W:(j + 1) * W] = jnp.zeros((W, W), BF)
    for u in range(KS):
        for diff, ref, flip in ((row_i - col_i + 4, w3, False), (col_i - row_i + 4, wt3, True)):
            band = jnp.zeros((W, W), F32)
            for v in range(KS):
                band = jnp.where(diff == v, kern_ref[u, fam, v], band)
            hi, lo = split(band)
            for d in range(5):
                for i in range(2):
                    for j in range(2):
                        if 2 * d + i - j == u:
                            a, b = (j, i) if flip else (i, j)
                            for k, val in ((0, hi), (1, hi), (2, lo)):
                                ref[d, (2 * k + a) * W:(2 * k + a + 1) * W, b * W:(b + 1) * W] = val

    def table(idx):
        def step(u, acc):
            for v in range(KS):
                acc = jnp.where(idx == u * KS + v, kern_ref[u, fam, v], acc)
            return acc
        hi, lo = split(lax.fori_loop(0, KS, step, jnp.zeros((W, W), F32)))
        return jnp.concatenate([hi, hi, lo], axis=0)

    def index(u, v, ok):
        good = ok & (u >= 0) & (u < KS) & (v >= 0) & (v < KS)
        return jnp.where(good, u * KS + v, -1)

    def strip_x(m):
        return jnp.where(m < 4, 128 + m, jnp.where(m < 8, 120 + m, jnp.where(m < 12, m - 8, m - 16)))

    m_row = row_i & 15
    cw = col_i & 7
    w_out = jnp.where(cw < 4, 124 + cw, cw - 4)
    for t in range(3):
        u = 8 * t + (row_i >> 4) - (col_i >> 3)
        v = strip_x(m_row) - w_out + 4
        fe3[t] = table(index(u, v, (m_row < 4) | (m_row >= 12)))
    x_in = jnp.where(m_row < 8, 120 + m_row, m_row - 8)
    for t in range(2):
        u = 8 * t + (col_i >> 4) - (row_i >> 4)
        v = strip_x(col_i & 15) - x_in + 4
        as3[t] = table(index(u, v, u == u))

    pl.semaphore_wait(barrier, nc - 1 + nr - 1 + sum(k[0].astype(jnp.int32) for k in corners))
    start(dg)
    first_side, _, first_rows, _ = ex(0)
    start(first_side)
    start(first_rows)


    qr, qc = iota((W, 2 * W), 0), iota((W, 2 * W), 1)
    q_sel[...] = jnp.where(qc == jnp.where(qr < C, qr, qr + C), 1.0, 0.0).astype(BF)
    m_t[...] = jnp.zeros_like(m_t)
    m_t[0:C, 0:bands] = m_ref[...]
    m_rows = jnp.transpose(m_t[...])
    gacc[0:full] = m_rows[0:full]
    gacc[full:] = jnp.zeros((BANDS - full, W), F32)
    gacc[BANDS - tail:] = m_rows[full:bands]
    low = iota((HALF, W), 1) < C
    md0 = gacc[...] + pltpu.roll(gacc[...], C, 1)
    blank = jnp.zeros((HALF - REST, W), F32)
    mp[0] = jnp.where(low, md0[0:HALF], jnp.concatenate([md0[HALF:], blank], axis=0))
    wgt[BANDS:] = jnp.zeros((HALF + 2 * span - BANDS, 2 * PAIRS * 2 * W), BF)
    for h in range(H):
        bend_v[h // 2, :, (h % 2) * W:(h % 2 + 1) * W] = jnp.broadcast_to(
            bend_ref[h:h + 1, :], (8, W)
        )

    def spectra_of(k):
        x = mp[k]
        y = pltpu.roll(x, C, 1)
        return jnp.concatenate([jnp.where(low, x, y), jnp.where(low, y, x)[0:REST]], axis=0)

    def set_spectra(k):
        hi, lo = split(spectra_of(k) * (1.0 / C))
        m_lhs[:, 0:W] = hi
        m_lhs[:, W:] = lo

    def set_transposed():
        mt_lhs[...] = mm_nt(q_sel[...], m_lhs[...]).astype(BF)

    for cp in o_cp:
        cp.wait()

    def many(ref, n, g, s_sem, r_sem, dr, dc):
        whole = ref.at[g, pl.ds(0, n)]
        return pltpu.make_async_remote_copy(
            src_ref=whole, dst_ref=whole, send_sem=s_sem.at[g], recv_sem=r_sem.at[g],
            device_id=(dr, dc), device_id_type=MESH,
        )

    next_c, next_r = lax.rem(c + 1, nc), lax.rem(r + 1, nr)

    def rs_many(n, g):
        return many(rs_buf, n, g, rs_s, rs_r, r, next_c)

    def b_many(g):
        return many(b_buf, nr - 1, g, b_s, b_r, next_r, c)

    def c_many(rows, g):
        whole = mp.at[g + 1, pl.ds(0, rows)]
        return pltpu.make_async_remote_copy(
            src_ref=whole, dst_ref=whole, send_sem=c_s.at[g], recv_sem=c_r.at[g],
            device_id=(r, next_c), device_id_type=MESH,
        )

    def chunk(k):
        return pl.ds(pl.multiple_of(k * rch, rch), rch)

    def rs_start(g, half):
        @pl.loop(0, grp)
        def _(j):
            k = half * grp + j

            @pl.when((k < nown) & (k != c))
            def _():
                pltpu.make_async_remote_copy(
                    src_ref=gp.at[g, chunk(k)], dst_ref=rs_buf.at[g, c],
                    send_sem=rs_s.at[g], recv_sem=rs_r.at[g],
                    device_id=(r, k), device_id_type=MESH,
                ).start()

    def b_start(g):
        @pl.when(owner)
        def _():
            rs_buf[g, c] = gp[g, chunk(c)]
            rs_many(nc - 1, g).wait_recv()
            total = rs_buf[g, 0]
            for j in range(1, nc):
                total = total + rs_buf[g, j]
            b_src[g] = total
            b_buf[g, r] = total

            @pl.loop(1, nr)
            def _(j):
                pltpu.make_async_remote_copy(
                    src_ref=b_src.at[g], dst_ref=b_buf.at[g, r],
                    send_sem=b_s.at[g], recv_sem=b_r.at[g],
                    device_id=(lax.rem(r + j, nr), c), device_id_type=MESH,
                ).start()

    def c_start(g):
        @pl.when(owner)
        def _():
            b_many(g).wait_recv()
            total = b_buf[g, 0]
            for j in range(1, nr):
                total = total + b_buf[g, j]
            mine = chunk(c)
            mp[g + 1, mine] = jnp.maximum(mp[g, mine] - 40.0 * (total / npix), 0.0)

            @pl.loop(1, nc)
            def _(j):
                pltpu.make_async_remote_copy(
                    src_ref=mp.at[g + 1, mine], dst_ref=mp.at[g + 1, mine],
                    send_sem=c_s.at[g], recv_sem=c_r.at[g],
                    device_id=(r, lax.rem(c + j, nc)), device_id_type=MESH,
                ).start()

    def c_wait(g):
        @pl.when(owner)
        def _():
            c_many((nown - 1) * rch, g).wait_recv()

        @pl.when(jnp.logical_not(owner))
        def _():
            c_many(nown * rch, g).wait_recv()

    def sent(g):
        @pl.when(owner)
        def _():
            rs_many(nown - 1, g).wait_send()
            b_many(g).wait_send()
            many(rs_buf, nc - 1, g, c_s, c_r, r, next_c).wait_send()

        @pl.when(jnp.logical_not(owner))
        def _():
            rs_many(nown, g).wait_send()

    lane_m = lane & 15
    lane_q = lane >> 4

    def lhs3(x):
        hi, lo = split(x)
        return jnp.concatenate([hi, lo, hi], axis=1)

    halo_lane = (lane_m < 4) | (lane_m >= 12)

    def sides_in(it):
        for t in range(3):
            left, right = r_side[it, 0, t], r_side[it, 1, t]
            x = jnp.where(lane_m >= 8, pltpu.roll(left, 8, 1), pltpu.roll(right, W - 8, 1))
            x_buf[t] = x
            if t != 1:
                v_buf[it, t // 2] = x + jnp.where(halo_lane, s_strip[it, t], 0.0)

    def update(it, t):
        x = x_buf[t]
        if t != 1:
            x = x + r_one[it, t // 2]
        total = s_strip[it, t] + x
        ok = ((lane_m < 4) & has_r) | ((lane_m >= 12) & has_l)
        if t == 0:
            ok = ok & ((lane_q >= 4) | has_up)
        if t == 2:
            ok = ok & ((lane_q < 4) | has_dn)
        a_strip[t] = jnp.maximum(a_strip[t] - 0.5 * jnp.where(ok, total, 0.0), 0.0)
        for i in range(4 * t, 4 * t + 4):
            for j in range(2):
                e = 2 * i + j
                sl = slice(j * W, (j + 1) * W)
                total = s_main[it, i, :, sl]
                if t == 0:
                    total = total + r_up[it, i, :, sl]
                if t == 2:
                    total = total + r_dn[it, i - (EXT - 4), :, sl]
                moved = pltpu.roll(x, (120 - 16 * (e % 8)) % W, 1)
                total = total + jnp.where(edge_lane, moved, 0.0)
                if e < 4:
                    total = jnp.where(has_up, total, 0.0)
                if e >= H + 4:
                    total = jnp.where(has_dn, total, 0.0)
                new = jnp.maximum(a_main[i, :, sl] - 0.5 * total, 0.0)
                a_main[i, :, sl] = new
                hi, lo = split(new)
                a3[i, :, j * W:(j + 1) * W] = hi
                a3[i, :, (2 + j) * W:(3 + j) * W] = lo
                a3[i, :, (4 + j) * W:(5 + j) * W] = hi

    def blocks(x, n):
        return x.reshape(n, C, 2 * W)

    def blur_inner():
        lhs = a3[4:8].reshape(4 * C, 6 * W)
        acc_b[4:8] = blocks(mm(lhs, w3[0]), 4)
        acc_b[0:4] = blocks(mm(lhs, w3[4]), 4)
        for d in (1, 2, 3):
            acc_b[4 - d:8 - d] += blocks(mm(lhs, w3[d]), 4)

    def blur_outer():
        for d in range(5):
            parts = []
            if d < 4:
                parts.append(a3[d:4].reshape((4 - d) * C, 6 * W))
            if d > 0:
                parts.append(a3[8:8 + d].reshape(d * C, 6 * W))
            res = mm(parts[0] if len(parts) == 1 else jnp.concatenate(parts, axis=0), w3[d])
            if d < 4:
                acc_b[0:4 - d] += blocks(res[0:(4 - d) * C], 4 - d)
            if d > 0:
                acc_b[8 - d:8] += blocks(res[(4 - d) * C:], d)
        edge = mm(lhs3(a_strip[0]), fe3[0]) + mm(lhs3(a_strip[1]), fe3[1]) + mm(lhs3(a_strip[2]), fe3[2])
        for p in range(PAIRS):
            for j in range(2):
                h = 2 * p + j
                moved = pltpu.roll(edge, (-8 * h - 4) % W, 1)
                val = acc_b[p, :, j * W:(j + 1) * W] + jnp.where(edge_lane, moved, 0.0)
                hi, lo = split(val)
                bb[0:C, h * W:(h + 1) * W] = hi
                bb[C:, h * W:(h + 1) * W] = lo

    def pair(p, k=0):
        lo = (k * PAIRS + p) * 2 * W
        return slice(lo, lo + 2 * W)

    def spectral():
        for p in range(PAIRS):
            both = bb[:, pair(p)]
            lin = mm(m_lhs[...], jnp.concatenate([both, both], axis=0))
            t = lin * bend_v[p, 0:1, :]
            a = 1.0 + t
            resid = lin * a - obs_v[p]
            hi, lo = split(resid * (a + t))
            wgt[0:BANDS, pair(p)] = hi
            wgt[0:BANDS, pair(p, 1)] = lo

    low_span = iota((span, W), 1) < C
    span_row = iota((span, W), 0)

    def spectra_grad(it, half):
        first, second = (
            pl.ds(pl.multiple_of(k * HALF + half * span, 16), span) for k in range(2)
        )
        n = PAIRS * 2 * W
        lhs = jnp.concatenate(
            [wgt[first, 0:n], wgt[second, 0:n], wgt[first, n:], wgt[second, n:]], axis=0
        )
        g = mm_nt(lhs, bb[...])
        g = g[0:2 * span] + g[2 * span:]
        g = (g + pltpu.roll(g, C, 1)) * (1.0 / C)
        parts = (g[0:span], g[span:])
        row = span_row + (half * span + HALF)
        second = jnp.where((row >= full) & (row < BANDS - tail), 0.0, parts[1])
        gp[it, pl.ds(pl.multiple_of(half * span, 8), span)] = jnp.where(low_span, parts[0], second)

    def pixel_grad():
        for p in range(PAIRS):
            part = mm(mt_lhs[...], wgt[0:BANDS, pair(p)]) + mm(mt_lhs[...], wgt[0:BANDS, pair(p, 1)])
            g = part[0:C] + part[C:]
            g_v[p] = g
            g3[p] = lhs3(g)

    def adjoint_strips(it):
        packed = []
        for t in range(2):
            acc = jnp.zeros((C, W), F32)
            for q in range(8):
                h = 8 * t + q
                row = g_v[h // 2, :, (h % 2) * W:(h % 2 + 1) * W]
                acc = jnp.where(lane_q == q, pltpu.roll(row, (16 * q + 8) % W, 1), acc)
            packed.append(lhs3(acc))
        s_strip[it, 0] = mm(packed[0], as3[0])
        s_strip[it, 1] = mm(packed[0], as3[1]) + mm(packed[1], as3[0])
        s_strip[it, 2] = mm(packed[1], as3[1])

    def adjoint_outer(it):
        for d in (0, 4, 1, 2, 3):
            parts = []
            if d < 4:
                parts.append(g3[0:4 - d].reshape((4 - d) * C, 6 * W))
            if d > 0:
                parts.append(g3[8 - d:8].reshape(d * C, 6 * W))
            res = mm(parts[0] if len(parts) == 1 else jnp.concatenate(parts, axis=0), wt3[d])
            if d == 0:
                s_main[it, 0:4] = blocks(res, 4)
            elif d == 4:
                s_main[it, 8:12] = blocks(res, 4)
            else:
                s_main[it, d:4] += blocks(res[0:(4 - d) * C], 4 - d)
                s_main[it, 8:8 + d] += blocks(res[(4 - d) * C:], d)

    def adjoint_inner(it):
        for d in range(5):
            res = blocks(mm(g3[4 - d:8 - d].reshape(4 * C, 6 * W), wt3[d]), 4)
            if d == 0:
                s_main[it, 4:8] = res
            else:
                s_main[it, 4:8] += res

    mine_half = c // grp

    @pl.loop(0, ITERS + 1)
    def _(it):
        side, rows_a, rows_b, ends = ex(it)
        more = it < ITERS

        @pl.when(it > 0)
        def _():
            b_start(it - 1)

        wait_recv(side)
        sides_in(it)
        start(ends)

        @pl.when(it > 0)
        def _():
            start(rows_b)

        update(it, 1)

        @pl.when(more)
        def _():
            blur_inner()

        @pl.when(it > 0)
        def _():
            c_start(it - 1)

        @pl.when(it == 0)
        def _():
            wait_recv(dg)
            for k in range(2):
                left, right = r_dg[2 * k], r_dg[2 * k + 1]
                r_one[0, k] = jnp.where(
                    lane_m >= 8, pltpu.roll(left, 8, 1), pltpu.roll(right, W - 8, 1)
                )

        wait_recv(ends)
        wait_recv(rows_a)
        wait_recv(rows_b)
        update(it, 0)
        update(it, 2)

        @pl.when(more)
        def _():
            blur_outer()

        @pl.when(jnp.logical_not(more))
        def _():
            a_out[...] = a_main[2:EXT - 2]

        @pl.when(it > 0)
        def _():
            c_wait(it - 1)

        @pl.when(more)
        def _():
            set_spectra(it)
            spectral()
            spectra_grad(it, 1 - mine_half)
            rs_start(it, 1 - mine_half)
            spectra_grad(it, mine_half)
            rs_start(it, mine_half)
            set_transposed()
            pixel_grad()
            adjoint_strips(it + 1)
            next_side, next_rows, _, _ = ex(it + 1)
            start(next_side)
            adjoint_outer(it + 1)
            start(next_rows)
            adjoint_inner(it + 1)

        wait_send(side)
        wait_send(rows_a)
        wait_send(rows_b)
        wait_send(ends)

        @pl.when(it > 0)
        def _():
            sent(it - 1)

    wait_send(dg)
    m_out[...] = mp[ITERS]


def finish(bands, a_ref, m_ref, a_hbm, mt_ref, m_v, sem):
    copies = [
        pltpu.make_async_copy(
            a_ref.at[h // 2, :, pl.ds((h % 2) * W, W)], a_hbm.at[:, h, :], sem.at[h]
        )
        for h in range(H)
    ]
    for cp in copies:
        cp.start()
    full = bands // 8 * 8
    tail = bands - full
    m_v[...] = jnp.zeros_like(m_v)
    m_v[0:HALF] = m_ref[...]
    m_v[HALF:BANDS] = pltpu.roll(m_ref[0:REST], C, 1)
    last = m_v[BANDS - tail:BANDS]
    m_v[full:bands] = last
    mt_ref[...] = jnp.transpose(m_v[...])[0:C, 0:bands]
    for cp in copies:
        cp.wait()


def solution(mesh):
    nr, nc = mesh.shape["rows"], mesh.shape["cols"]
    rch, _ = chunks(nc)

    def on_device(observed, nonlin, abundance, spectra, kernels, tile_family):
        bands = observed.shape[0]
        vm = pltpu.VMEM
        dma = pltpu.SemaphoreType.DMA
        scratch = [
            vm((PAIRS, BANDS, 2 * W), F32), vm((PAIRS, C, 2 * W), F32), vm((PAIRS, 8, 2 * W), F32),
            vm((4, EXT, C, 2 * W), F32), vm((4, 3, C, W), F32),
            vm((EXT, C, 2 * W), F32), vm((3, C, W), F32), vm((EXT, C, 6 * W), BF),
            vm((4, 4, C, 2 * W), F32), vm((4, 4, C, 2 * W), F32), vm((4, 2, C, W), F32),
            vm((4, 2, 3, C, W), F32), vm((4, C, W), F32), vm((4, 2, C, W), F32), vm((3, C, W), F32),
            vm((5, 6 * W, 2 * W), BF), vm((5, 6 * W, 2 * W), BF),
            vm((3, 3 * W, W), BF), vm((2, 3 * W, W), BF),
            vm((PAIRS, C, 2 * W), F32), vm((2 * C, PAIRS * 2 * W), BF),
            vm((HALF + nc // 2 * rch * 2, 2 * PAIRS * 2 * W), BF),
            vm((PAIRS, C, 2 * W), F32), vm((PAIRS, C, 6 * W), BF),
            vm((BANDS, W), F32), vm((BANDS, 2 * W), BF), vm((W, BANDS), BF), vm((W, 2 * W), BF),
            vm((W, 4 * W), F32),
            vm((ITERS, nc // 2 * rch * 2, W), F32), vm((ITERS, nc, rch, W), F32), vm((ITERS, rch, W), F32),
            vm((ITERS, nr, rch, W), F32), vm((ITERS + 1, HALF, W), F32),
            dma((3, H)), dma((4, 8)), dma((4, 8)), dma((4,)), dma((4,)),
            dma((ITERS,)), dma((ITERS,)), dma((ITERS,)), dma((ITERS,)), dma((ITERS,)), dma((ITERS,)),
        ]
        def held(x):
            return pltpu.with_memory_space_constraint(x, pltpu.HBM)

        any_spec = pl.BlockSpec(memory_space=pltpu.HBM)
        vspec = pl.BlockSpec(memory_space=pltpu.VMEM)
        sspec = pl.BlockSpec(memory_space=pltpu.SMEM)
        out, m_out = pl.pallas_call(
            functools.partial(kernel, nr, nc, bands),
            out_shape=(
                jax.ShapeDtypeStruct((PAIRS, C, 2 * W), F32),
                jax.ShapeDtypeStruct((HALF, W), F32),
            ),
            in_specs=[any_spec, vspec, any_spec, vspec, sspec, sspec],
            out_specs=(vspec, vspec),
            scratch_shapes=scratch,
            compiler_params=pltpu.CompilerParams(collective_id=0, has_side_effects=True, vmem_limit_bytes=VM_LIMIT),
            name="unmix",
        )(held(observed), held(nonlin), held(abundance), held(spectra.T), held(jnp.transpose(kernels, (1, 0, 2))), tile_family)
        out, m_out = pl.pallas_call(
            functools.partial(finish, bands),
            out_shape=(
                jax.ShapeDtypeStruct(abundance.shape, F32),
                jax.ShapeDtypeStruct((C, bands), F32),
            ),
            in_specs=[vspec, vspec],
            out_specs=(pl.BlockSpec(memory_space=pltpu.HBM), vspec),
            scratch_shapes=[vm((4 * W, W), F32), dma((H,))],
            compiler_params=pltpu.CompilerParams(vmem_limit_bytes=8 * 1024 * 1024),
            name="finish",
        )(out, m_out)
        return out, m_out.T

    placed = (
        P(None, "rows", "cols"), P("rows", "cols"), P(None, "rows", "cols"),
        P(), P(), P("rows", "cols"),
    )
    return jax.shard_map(
        on_device, mesh=mesh, in_specs=placed,
        out_specs=(P(None, "rows", "cols"), P()), check_vma=False,
    )
```
